256 devices in a mesh: gx: 8 (over y, x_lo), gy: 32 (over x_hi, z, core).
Axes of the slice: x: 4 (x_hi: 2, x_lo: 2; x = x_hi * 2 + x_lo), y: 4, z: 8, core: 2. Of those that a mesh axis runs over, the one named last changes fastest.
Arguments:
- u_vel: float32 [8, 4096, 4096], P(None, 'gx', 'gy'), may hold values from -6 to 6
- v_vel: float32 [8, 4096, 4096], P(None, 'gx', 'gy'), may hold values from -6 to 6
- w_vel: float32 [8, 4096, 4096], P(None, 'gx', 'gy'), may hold values from -6 to 6
- thickness: float32 [8], replicated, may hold values from 128 to 512
Outputs:
- u_out: float32 [8, 4096, 4096], P(None, 'gx', 'gy')
- v_out: float32 [8, 4096, 4096], P(None, 'gx', 'gy')
- w_out: float32 [8, 4096, 4096], P(None, 'gx', 'gy')
The draws below stay inside these ranges and needn't reach their ends.
All inputs are finite; a program needn't handle non-finite values.
Results may differ from the reference program's by a relative error of at most 0.0003.
Values sent between devices are 32-bit elements; how exact they have to be, the bound alone decides.
No kernel may reach another device: no remote copies, remote signals or barrier semaphores. Data moves between devices by JAX's collectives and lax.ppermute only.
A program may use at most 128 MiB of HBM per device.

```python
import math
import jax
import jax.numpy as jnp
from jax import lax

NX = 4096
NY = 4096
NZ = 8


def levels(rng, extent, cuts, low, largest):
    factor_of = 1.0
    for dim, blocks in cuts:
        heights = jax.random.uniform(jax.random.fold_in(jax.random.fold_in(rng, 6), dim), (blocks,), jnp.float32, low / len(cuts), largest / len(cuts))
        factor_of = factor_of * jnp.repeat(jnp.exp(heights), extent[dim] // blocks).reshape((-1,) + (1,) * (len(extent) - 1 - dim))
    return factor_of


def noise(own_key, shape, deviation, limit, cuts=(), held_as=jnp.bfloat16):
    drawn = deviation * jax.random.normal(own_key, shape, jnp.float32)
    if cuts:
        drawn = drawn * levels(own_key, shape, cuts, -0.22, 0.18)
    return jnp.clip(drawn, -limit, limit).astype(held_as)


def setup_inputs(seed: int = 0) -> dict:
    key_list = jax.random.split(jax.random.key(seed), 5)
    return {
        "u_vel": noise(key_list[0], (NZ, NX, NY), 1.0, 6.0, ((1, 8), (2, 32)), jnp.float32),
        "v_vel": noise(key_list[1], (NZ, NX, NY), 1.0, 6.0, ((1, 8), (2, 32)), jnp.float32),
        "w_vel": noise(key_list[2], (NZ, NX, NY), 1.0, 6.0, ((1, 8), (2, 32)), jnp.float32),
        "thickness": jnp.clip(jnp.exp(jax.random.uniform(key_list[3], (NZ,), jnp.float32, math.log(128.0), math.log(512.0))), 128.0, 512.0),
    }


def level_solve(rhs, wave_x, wave_y, thickness, width_x, width_y):
    lam_x = -4.0 * jnp.sin(wave_x.astype(jnp.float32) * (math.pi / (2 * width_x))) ** 2
    lam_y = -4.0 * jnp.sin(wave_y.astype(jnp.float32) * (math.pi / width_y)) ** 2
    eigen = lam_x[:, None] + lam_y[None, :]
    ground = ((wave_x == 0)[:, None] & (wave_y == 0)[None, :]).astype(jnp.float32)
    centre = 0.5 * (thickness[:-1] + thickness[1:])
    upper = jnp.concatenate([1.0 / (thickness[:-1] * centre), jnp.zeros((1,), jnp.float32)])
    lower = jnp.concatenate([jnp.zeros((1,), jnp.float32), 1.0 / (thickness[1:] * centre)])
    above = jnp.concatenate([jnp.ones((1,), jnp.float32), upper[:-1]])
    pinned = jnp.concatenate([upper[:1], jnp.zeros((thickness.shape[0] - 1,), jnp.float32)])

    def sweep(carry, level):
        excess_prev, reduced_prev = carry
        lower_k, upper_k, above_k, pin_k, rhs_k = level
        excess = eigen - pin_k * ground + lower_k * excess_prev / (above_k - excess_prev)
        pivot_value = excess - upper_k
        reduced = (rhs_k - lower_k * reduced_prev) / pivot_value
        return (excess, reduced), (reduced, upper_k / pivot_value)

    zeros_plane = jnp.zeros(eigen.shape, jnp.float32)
    unused, (reduced_all, ratio_all) = lax.scan(sweep, (zeros_plane, zeros_plane), (lower, upper, above, pinned, rhs))

    def backward(carry, level):
        reduced, ratio = level
        value = reduced - ratio * carry
        return value, value

    unused_last, solved = lax.scan(backward, zeros_plane, (reduced_all, ratio_all), reverse=True)
    scale = jnp.where(wave_x == 0, 1.0 / width_x, 2.0 / width_x).astype(jnp.float32)[:, None] / width_y
    return solved * scale


def reference(u_vel, v_vel, w_vel, thickness):
    zero_x = jnp.zeros((NZ, 1, NY), jnp.float32)
    zero_z = jnp.zeros((1, NX, NY), jnp.float32)
    at_wall = (jnp.arange(NX, dtype=jnp.int32) == NX - 1)[None, :, None]
    u_open = jnp.where(at_wall, jnp.zeros((), jnp.float32), u_vel)
    u_prev = jnp.concatenate([zero_x, u_open[:, :-1, :]], axis=1)
    v_prev = jnp.roll(v_vel, 1, axis=2)
    w_open = jnp.concatenate([w_vel[:-1], zero_z], axis=0)
    w_prev = jnp.concatenate([zero_z, w_open[:-1]], axis=0)
    divergence = (u_open - u_prev) + (v_vel - v_prev) + (w_open - w_prev) / thickness[:, None, None]
    angle = jnp.arange(NX, dtype=jnp.float32) * (math.pi / (2 * NX))
    cos_fold = jnp.cos(angle)[:, None]
    sin_fold = jnp.sin(angle)[:, None]

    def forward_level(level):
        folded = jnp.concatenate([level[0::2], jnp.flip(level[1::2], axis=0)], axis=0)
        spectrum = jnp.fft.fft(folded, axis=0)
        along_x = spectrum.real * cos_fold + spectrum.imag * sin_fold
        spec_y = jnp.fft.fft(along_x, axis=1)
        return spec_y.real - spec_y.imag

    rhs_hat = lax.map(forward_level, divergence)
    wave_x = jnp.arange(NX, dtype=jnp.int32)
    wave_y = jnp.arange(NY, dtype=jnp.int32)
    pressure_hat = level_solve(rhs_hat, wave_x, wave_y, thickness, NX, NY)

    def inverse_level(level):
        spec_y = jnp.fft.fft(level, axis=1)
        rows = spec_y.real - spec_y.imag
        mixed = jnp.fft.fft(lax.complex(rows * cos_fold, -(rows * sin_fold)), axis=0).real
        half = NX // 2
        evens = mixed[:half]
        odds = jnp.flip(mixed[half:], axis=0)
        return jnp.stack([evens, odds], axis=1).reshape(NX, NY)

    pressure = lax.map(inverse_level, pressure_hat)
    next_x = jnp.concatenate([pressure[:, 1:, :], zero_x], axis=1)
    next_y = jnp.roll(pressure, -1, axis=2)
    next_z = jnp.concatenate([pressure[1:], zero_z], axis=0)
    centre = 0.5 * (thickness[:-1] + thickness[1:])
    spacing = jnp.concatenate([centre, jnp.ones((1,), jnp.float32)])
    u_out = jnp.where(at_wall, jnp.zeros((), jnp.float32), u_vel - (next_x - pressure))
    v_out = v_vel - (next_y - pressure)
    top = (jnp.arange(NZ, dtype=jnp.int32) == NZ - 1)[:, None, None]
    w_out = jnp.where(top, jnp.zeros((), jnp.float32), w_vel - (next_z - pressure) / spacing[:, None, None])
    return u_out, v_out, w_out
```

```python
import math

import jax
import jax.numpy as jnp
import numpy as np
from jax import lax
from jax.experimental import pallas as pl
from jax.experimental.pallas import tpu as pltpu
from jax.sharding import PartitionSpec as P

highest = lax.Precision.HIGHEST
f32 = jnp.float32
NX = 4096
NY = 4096
NZ = 8
LX = 512
ROWS = 136
PAY = 520
HALF = float(np.sqrt(0.5))

CLASSES = [0] + [mu + 16 * tau for mu in range(1, 8) for tau in range(4)] + [16, 8, 24]


def class_modes():
    t = np.arange(64)
    rows = [np.concatenate([64 * t, 64 * t + 32])]
    for nu in CLASSES[1:]:
        rows.append(np.concatenate([64 * t + nu, 64 * (t + 1) - nu]))
    return np.stack(rows)


def dct_tables():
    b = np.arange(128)[:, None]
    t = np.arange(64)[None, :]
    near = math.pi * t * (2 * b + 1) / 128
    far = math.pi * (t + 1) * (2 * b + 1) / 128
    common = np.block([[np.cos(near), np.cos(far)], [np.sin(near), -np.sin(far)]])
    zero = np.zeros((128, 64))
    middle = np.cos(math.pi * (64 * t + 32) * (2 * b + 1) / 8192)
    first = np.block([[np.cos(near), zero], [zero, middle]])
    nu = np.array(CLASSES)[:, None]
    angle = math.pi * nu * (2 * np.arange(128)[None, :] + 1) / 8192
    return common, first, np.cos(angle), np.sin(angle)


def line_tables():
    d = np.arange(32)
    j = np.arange(128)
    a32 = 2 * math.pi * (d[:, None] * d[None, :] % 32) / 32
    a128 = 2 * math.pi * (j[:, None] * j[None, :] % 128) / 128
    tw = 2 * math.pi * (d[:, None] * j[None, :]) / 4096
    q = d[:, None] + 32 * j[None, :]
    lam = -4.0 * np.sin(math.pi * q / NY) ** 2
    return np.cos(a32), np.sin(a32), np.cos(tw), np.sin(tw), np.cos(a128), np.sin(a128), lam


def const(values):
    return jnp.asarray(np.asarray(values, dtype=np.float32))


def across_blocks(x):
    e = [x[s] + x[s + 4] for s in range(4)]
    o = [x[s] - x[s + 4] for s in range(4)]
    out = [None] * 9
    e02, e13 = e[0] + e[2], e[1] + e[3]
    out[0] = e02 + e13
    out[8] = e02 - e13
    out[4] = (e[0] - e[2], e[3] - e[1])
    d13, s13 = HALF * (o[1] - o[3]), HALF * (o[1] + o[3])
    out[2] = (o[0] + d13, -o[2] - s13)
    out[6] = (o[0] - d13, o[2] - s13)
    zr, zi = [x[0]], [-x[4]]
    for s in (1, 2, 3):
        c, q = math.cos(math.pi * s / 8), math.sin(math.pi * s / 8)
        zr.append(x[s] * c - x[s + 4] * q)
        zi.append(-(x[s] * q + x[s + 4] * c))
    y = four(zr, zi)
    out[1] = y[0]
    out[5] = y[1]
    out[7] = (y[2][0], -y[2][1])
    out[3] = (y[3][0], -y[3][1])
    return out


def four(zr, zi):
    t0r, t0i = zr[0] + zr[2], zi[0] + zi[2]
    t1r, t1i = zr[0] - zr[2], zi[0] - zi[2]
    t2r, t2i = zr[1] + zr[3], zi[1] + zi[3]
    t3r, t3i = zr[1] - zr[3], zi[1] - zi[3]
    return [
        (t0r + t2r, t0i + t2i),
        (t1r + t3i, t1i - t3r),
        (t0r - t2r, t0i - t2i),
        (t1r - t3i, t1i + t3r),
    ]


def four_back(h):
    zr = [v[0] for v in h]
    zi = [v[1] for v in h]
    t0r, t0i = zr[0] + zr[2], zi[0] + zi[2]
    t1r, t1i = zr[0] - zr[2], zi[0] - zi[2]
    t2r, t2i = zr[1] + zr[3], zi[1] + zi[3]
    t3r, t3i = zr[1] - zr[3], zi[1] - zi[3]
    return [
        (t0r + t2r, t0i + t2i),
        (t1r - t3i, t1i + t3r),
        (t0r - t2r, t0i - t2i),
        (t1r + t3i, t1i - t3r),
    ]


def forward_classes(x):
    per_a = [across_blocks([x[4 * s + a] for s in range(8)]) for a in range(4)]
    out = []
    y0 = [per_a[a][0] for a in range(4)]
    y8 = [per_a[a][8] for a in range(4)]
    out.append(((y0[0] + y0[2]) + (y0[1] + y0[3]), (y0[0] + y0[2]) - (y0[1] + y0[3])))
    for mu in range(1, 8):
        zr, zi = [per_a[0][mu][0]], [per_a[0][mu][1]]
        for a in (1, 2, 3):
            yr, yi = per_a[a][mu]
            c, q = math.cos(math.pi * mu * a / 32), math.sin(math.pi * mu * a / 32)
            zr.append(yr * c + yi * q)
            zi.append(yi * c - yr * q)
        out.extend(four(zr, zi))
    out.append((y0[0] - y0[2], y0[3] - y0[1]))
    d13, s13 = HALF * (y8[1] - y8[3]), HALF * (y8[1] + y8[3])
    out.append((y8[0] + d13, -y8[2] - s13))
    out.append((y8[0] - d13, y8[2] - s13))
    return out


def backward_classes(h):
    h0, h32 = h[0]
    h16, h8, h24 = h[29], h[30], h[31]
    x = [None] * 32
    by_mu = {}
    for mu in range(1, 8):
        z = four_back(h[1 + 4 * (mu - 1) : 5 + 4 * (mu - 1)])
        for a in (1, 2, 3):
            c, q = math.cos(math.pi * mu * a / 32), math.sin(math.pi * mu * a / 32)
            zr, zi = z[a]
            z[a] = (zr * c - zi * q, zr * q + zi * c)
        by_mu[mu] = z
    sum0, dif0 = h0 + h32, h0 - h32
    y0 = [sum0 + h16[0], dif0 - h16[1], sum0 - h16[0], dif0 + h16[1]]
    dr, di = HALF * (h8[0] - h24[0]), HALF * (h8[1] + h24[1])
    y8 = [h8[0] + h24[0], dr - di, h24[1] - h8[1], -dr - di]
    for a in range(4):
        y = {mu: by_mu[mu][a] for mu in by_mu}
        ea, eb = y0[a] + y8[a], y0[a] - y8[a]
        y2, y4, y6 = y[2], y[4], y[6]
        rep = [ea + y4[0], eb - y4[1], ea - y4[0], eb + y4[1]]
        er, ei = HALF * (y2[0] - y6[0]), HALF * (y2[1] + y6[1])
        alt = [y2[0] + y6[0], er - ei, y6[1] - y2[1], -er - ei]
        u = four_back([y[1], y[5], (y[7][0], -y[7][1]), (y[3][0], -y[3][1])])
        for s in range(4):
            ur, ui = u[s]
            if s:
                c, q = math.cos(math.pi * s / 8), math.sin(math.pi * s / 8)
                ur, ui = ur * c - ui * q, ur * q + ui * c
            x[4 * s + a] = rep[s] + alt[s] + ur
            x[4 * (s + 4) + a] = rep[s] - alt[s] - ui
    return x


def decay(eigen):
    half = 0.5 * jnp.sqrt(-eigen)
    root = jnp.sqrt(1.0 + half * half)
    gap = 2.0 * half * (root - half)
    return 1.0 - gap, gap, -0.25 / (half * root)


def doubled(gap, times):
    for _ in range(times):
        gap = gap * (2.0 - gap)
    return gap


ROUNDS = []
_seats = list(range(8))
for _ in range(7):
    ROUNDS.append([tuple(sorted((_seats[i], _seats[7 - i]))) for i in range(4)])
    _seats = [_seats[0], _seats[7]] + _seats[1:7]
SWEEPS = 6
PAIRS = [(i, j) for i in range(8) for j in range(i, 8)]


def vertical_modes(thick_ref, mix_ref, unmix_ref, mu_ref):
    t = [jnp.full((8, 128), thick_ref[k], f32) for k in range(8)]
    unit = 16384.0
    zero = jnp.zeros((8, 128), f32)
    one = jnp.ones((8, 128), f32)
    centre = [0.5 * (t[k] + t[k + 1]) for k in range(7)]
    root = [jnp.sqrt(t[k]) for k in range(8)]
    a = {pair: zero for pair in PAIRS}
    for k in range(8):
        total = zero
        if k < 7:
            total = total + unit / (t[k] * centre[k])
            a[(k, k + 1)] = unit / (centre[k] * (root[k] * root[k + 1]))
        if k > 0:
            total = total + unit / (t[k] * centre[k - 1])
        a[(k, k)] = -total
    vec = [[one if i == j else zero for j in range(8)] for i in range(8)]

    def sweep(_, carry):
        flat_a, flat_v = carry
        a = dict(zip(PAIRS, flat_a))
        vec = [list(flat_v[8 * i : 8 * i + 8]) for i in range(8)]

        def get(i, j):
            return a[(i, j) if i <= j else (j, i)]

        for pairs in ROUNDS:
            turn = {}
            for p, q in pairs:
                off = a[(p, q)]
                diff = a[(q, q)] - a[(p, p)]
                size = jnp.sqrt(diff * diff + 4.0 * off * off)
                low = jnp.where(diff < 0.0, diff - size, diff + size)
                tan = 2.0 * off / jnp.where(low == 0.0, 1.0, low)
                cos = 1.0 / jnp.sqrt(1.0 + tan * tan)
                turn[(p, q)] = (cos, tan * cos, tan)
            full = [[get(i, j) for j in range(8)] for i in range(8)]
            for p, q in pairs:
                cos, sin, _t = turn[(p, q)]
                for i in range(8):
                    x, y = full[i][p], full[i][q]
                    full[i][p], full[i][q] = cos * x - sin * y, sin * x + cos * y
                    x, y = vec[i][p], vec[i][q]
                    vec[i][p], vec[i][q] = cos * x - sin * y, sin * x + cos * y
            for p, q in pairs:
                cos, sin, tan = turn[(p, q)]
                for j in range(8):
                    x, y = full[p][j], full[q][j]
                    full[p][j], full[q][j] = cos * x - sin * y, sin * x + cos * y
            diag = {}
            for p, q in pairs:
                cos, sin, tan = turn[(p, q)]
                off = a[(p, q)]
                diag[p] = a[(p, p)] - tan * off
                diag[q] = a[(q, q)] + tan * off
            a = {(i, j): full[i][j] for i, j in PAIRS}
            for p, q in pairs:
                a[(p, q)] = zero
            for p in diag:
                a[(p, p)] = diag[p]
        return tuple(a[pair] for pair in PAIRS), tuple(vec[i][j] for i in range(8) for j in range(8))

    start = (tuple(a[pair] for pair in PAIRS), tuple(vec[i][j] for i in range(8) for j in range(8)))
    flat_a, flat_v = lax.fori_loop(0, SWEEPS, sweep, start)
    a = dict(zip(PAIRS, flat_a))
    for mode in range(8):
        mu_ref[mode : mode + 1, :] = jnp.minimum(a[(mode, mode)] * (1.0 / unit), 0.0)[0:1]
        for k in range(8):
            entry = flat_v[8 * k + mode]
            mix_ref[8 * mode + k : 8 * mode + k + 1, :] = (entry * root[k])[0:1]
            unmix_ref[8 * k + mode : 8 * k + mode + 1, :] = (entry / root[k])[0:1]


def iota(shape, axis):
    return lax.broadcasted_iota(jnp.int32, shape, axis)


def divergence_kernel(gx_ref, thick_ref, mix_ref, u_ref, v_ref, w_ref, out_ref, last_ref, sum_ref):
    step = pl.program_id(0)
    wall = jnp.logical_and(gx_ref[0] == 7, step == 3)

    @pl.when(step == 0)
    def _():
        last_ref[...] = jnp.zeros((64, 128), f32)
        sum_ref[...] = jnp.zeros((64, 128), f32)

    lane = iota((16, 128), 1)
    row = iota((16, 128), 0)
    ones = jnp.ones((1, 128), f32)
    inverse = [1.0 / (ones * thick_ref[k]) for k in range(8)]
    base = pl.multiple_of(step * 128, 128)
    for sub in range(8):
        rows = slice(16 * sub, 16 * sub + 16)
        div = []
        below = None
        for k in range(8):
            u = u_ref[k, rows, :]
            if sub == 7:
                u = jnp.where(jnp.logical_and(wall, row == 15), 0.0, u)
            prev = pltpu.roll(u, 1, axis=0)
            prev = jnp.where(row == 0, last_ref[8 * k : 8 * k + 1, :], prev)
            last_ref[8 * k : 8 * k + 1, :] = u[15:16]
            v = v_ref[k, rows, :]
            back = jnp.where(lane == 0, 0.0, pltpu.roll(v, 1, axis=1))
            if k < 7:
                w = w_ref[k, rows, :]
                up = w if below is None else w - below
                below = w
            else:
                up = -below
            rise = up * inverse[k]
            sum_ref[8 * k : 8 * k + 8, :] += rise[0:8] + rise[8:16]
            div.append((u - prev) + (v - back) + rise)
        for mode in range(8):
            acc = div[0] * mix_ref[8 * mode : 8 * mode + 1, :]
            for k in range(1, 8):
                acc = acc + div[k] * mix_ref[8 * mode + k : 8 * mode + k + 1, :]
            out_ref[mode, pl.ds(base + 16 * sub, 16), :] = acc

    lanes = iota((128, 128), 1)
    edge = jnp.zeros((128, 128), f32)
    for k in range(8):
        edge = jnp.where(lanes == k, pltpu.roll(v_ref[k], k + 1, axis=1), edge)
    edge = edge.T
    for mode in range(8):
        acc = edge[0:1] * mix_ref[8 * mode : 8 * mode + 1, :]
        for k in range(1, 8):
            acc = acc + edge[k : k + 1] * mix_ref[8 * mode + k : 8 * mode + k + 1, :]
        out_ref[mode, pl.ds(513 + step, 1), :] = -acc

    @pl.when(step == 3)
    def _():
        lane1 = iota((1, 128), 1)
        totals = jnp.zeros((1, 128), f32)
        for k in range(8):
            part = jnp.sum(sum_ref[8 * k : 8 * k + 8, :], axis=0, keepdims=True)
            part = jnp.sum(part, axis=1, keepdims=True)
            totals = jnp.where(lane1 == k, part, totals)
        for mode in range(8):
            acc = last_ref[0:1, :] * mix_ref[8 * mode : 8 * mode + 1, :]
            for k in range(1, 8):
                acc = acc + last_ref[8 * k : 8 * k + 1, :] * mix_ref[8 * mode + k : 8 * mode + k + 1, :]
            out_ref[mode, 512:513, :] = acc
            out_ref[mode, 517:518, :] = totals
            out_ref[mode, 518:520, :] = jnp.zeros((2, 128), f32)


def eigen_table(sines, mu_row, with_first):
    eigen = mu_row - 4.0 * sines
    if with_first:
        first = jnp.logical_and(iota(sines.shape, 0) == 0, iota(sines.shape, 1) == 0)
        eigen = jnp.where(first, -1.0, eigen)
    return eigen


def forward_kernel(
    gx_ref, mu_ref, sines_ref, tc_ref, ts_ref, common_ref, first_ref, in_ref, out_ref, small_ref,
    grid_ref, y_ref, side_ref,
):
    row8 = iota((8, 128), 0)
    row128 = iota((128, 128), 0)
    for s in range(8):
        for part in range(4):
            tile = in_ref[s, 128 * part : 128 * part + 128, :]
            if part == 0 and s > 0:
                tile = jnp.where(row128 == 0, tile - in_ref[s - 1, 512:513, :], tile)
            grid_ref[4 * s + part, 0:128, :] = tile.T
            ghost = in_ref[s, 513 + part : 514 + part, :]
            grid_ref[4 * s + part, 128:136, :] = jnp.where(row8 == 0, ghost, 0.0)

    def group(i, carry):
        start = pl.multiple_of(i * 8, 8)
        rows = pl.ds(start, 8)
        y = forward_classes([grid_ref[g, rows, :] for g in range(32)])
        y_ref[0, rows, 0:128] = y[0][0]
        y_ref[0, rows, 128:256] = y[0][1]
        for c in range(1, 32):
            re, im = y[c]
            tc, ts = tc_ref[c : c + 1, :], ts_ref[c : c + 1, :]
            y_ref[c, rows, 0:128] = re * tc + im * ts
            y_ref[c, rows, 128:256] = im * tc - re * ts
        return carry

    lax.fori_loop(0, ROWS // 8, group, 0)

    out_ref[0:ROWS, :] = jnp.dot(y_ref[0], first_ref[...], precision=highest, preferred_element_type=f32)

    def product(c, carry):
        start = pl.multiple_of(c * ROWS, 8)
        out_ref[pl.ds(start, ROWS), :] = jnp.dot(
            y_ref[c], common_ref[...], precision=highest, preferred_element_type=f32
        )
        return carry

    lax.fori_loop(1, 32, product, 0)

    line = out_ref[0:128, :].T[0:1]
    ghost_line = out_ref[128:129, :]

    eigen = eigen_table(sines_ref[...], mu_ref[pl.ds(gx_ref[0], 1), :], True)
    rho, gap, _ = decay(eigen)
    ghost = out_ref[pl.ds(128, 32, stride=ROWS), :]

    def from_north(n, b):
        j = 127 - n
        side_ref[pl.ds(j, 32, stride=ROWS), :] = rho * b
        return out_ref[pl.ds(j, 32, stride=ROWS), :] + (b - gap * b)

    b = lax.fori_loop(0, 128, from_north, ghost, unroll=8)

    def from_south(j, f):
        f = out_ref[pl.ds(j, 32, stride=ROWS), :] + (f - gap * f)
        out_ref[pl.ds(j, 32, stride=ROWS), :] = f + side_ref[pl.ds(j, 32, stride=ROWS), :]
        return f

    f = lax.fori_loop(0, 128, from_south, jnp.zeros((32, 128), f32), unroll=8)
    out_ref[pl.ds(128, 32, stride=ROWS), :] = rho * f + ghost

    totals = in_ref[0, 517:518, :]
    for s in range(1, 8):
        totals = totals + in_ref[s, 517:518, :]
    small_ref[pl.ds(0, 32, stride=8), :] = f + ghost / rho
    small_ref[pl.ds(1, 32, stride=8), :] = b
    small_ref[pl.ds(2, 32, stride=8), :] = jnp.broadcast_to(line, (32, 128))
    small_ref[pl.ds(3, 32, stride=8), :] = jnp.broadcast_to(totals, (32, 128))
    small_ref[pl.ds(4, 32, stride=8), :] = jnp.broadcast_to(ghost_line, (32, 128))
    for r in (5, 6, 7):
        small_ref[pl.ds(r, 32, stride=8), :] = jnp.zeros((32, 128), f32)


def carry_kernel(gx_ref, gy_ref, mu_ref, sines_ref, in_ref, out_ref):
    own = gy_ref[0]
    eigen = mu_ref[pl.ds(gx_ref[0], 1), :] - 4.0 * sines_ref[pl.ds(own, 1), :]
    first = jnp.logical_and(own == 0, iota((1, 128), 1) == 0)
    eigen = jnp.where(first, -1.0, eigen)
    _, gap, _ = decay(eigen)
    gap_block = doubled(gap, 7)
    around = 1.0 / doubled(gap_block, 5)
    c = jnp.zeros((1, 128), f32)
    h = jnp.zeros((1, 128), f32)
    for d in range(32):
        c = in_ref[8 * d : 8 * d + 1, :] + (c - gap_block * c)
        e = 31 - d
        h = in_ref[8 * e + 1 : 8 * e + 2, :] + (h - gap_block * h)
    c = c * around
    h = h * around
    out_ref[...] = jnp.zeros((256, 128), f32)
    for d in range(32):
        out_ref[8 * d : 8 * d + 1, :] = c
        c = in_ref[8 * d : 8 * d + 1, :] + (c - gap_block * c)
        e = 31 - d
        out_ref[8 * e + 1 : 8 * e + 2, :] = h
        h = in_ref[8 * e + 1 : 8 * e + 2, :] + (h - gap_block * h)


def line_kernel(
    gx_ref, thick_ref, mu_ref, c32_ref, s32_ref, tc_ref, ts_ref, c128_ref, s128_ref, lam_ref,
    in_ref, out_ref,
):
    def times(a, b):
        return jnp.dot(a, b, precision=highest, preferred_element_type=f32)

    line = in_ref[pl.ds(2, 32, stride=8), :]
    ghost = in_ref[pl.ds(4, 32, stride=8), :]
    at_first = iota((32, 128), 1) == 0
    line = line + jnp.where(at_first, pltpu.roll(ghost, 1, axis=0), 0.0)
    c32, s32 = c32_ref[...], s32_ref[...]
    tc, ts = tc_ref[...], ts_ref[...]
    c128, s128 = c128_ref[...], s128_ref[...]
    re, im = times(c32, line), -times(s32, line)
    re, im = re * tc + im * ts, im * tc - re * ts
    re, im = times(re, c128) + times(im, s128), times(im, c128) - times(re, s128)
    mean = jnp.logical_and(iota((32, 128), 0) == 0, at_first)
    eigen = mu_ref[pl.ds(gx_ref[0], 1), :] + lam_ref[...]
    gain = jnp.where(mean, 0.0, (1.0 / NY) / jnp.where(mean, 1.0, eigen))
    re, im = re * gain, im * gain
    re, im = times(re, c128) - times(im, s128), times(im, c128) + times(re, s128)
    re, im = re * tc - im * ts, im * tc + re * ts
    out_ref[0:32, :] = times(c32, re) - times(s32, im)

    totals = jnp.sum(in_ref[pl.ds(3, 32, stride=8), :], axis=0, keepdims=True)
    lane = iota((1, 128), 1)
    ones = jnp.ones((1, 128), f32)
    rhs = [ones * jnp.sum(jnp.where(lane == k, totals, 0.0), axis=1, keepdims=True) for k in range(8)]
    t = [ones * thick_ref[k] for k in range(8)]
    centre = [0.5 * (t[k] + t[k + 1]) for k in range(7)]
    zero = jnp.zeros((1, 128), f32)
    upper = [1.0 / (t[k] * centre[k]) for k in range(7)] + [zero]
    lower = [zero] + [1.0 / (t[k] * centre[k - 1]) for k in range(1, 8)]
    reduced, ratio = [], []
    excess = zero
    for k in range(8):
        if k == 0:
            excess = -upper[0]
            top = rhs[0]
        else:
            excess = lower[k] * excess / (upper[k - 1] - excess)
            top = rhs[k] - lower[k] * reduced[-1]
        pivot = excess - upper[k]
        reduced.append(top / pivot)
        ratio.append(upper[k] / pivot)
    value = zero
    for k in reversed(range(8)):
        value = reduced[k] - ratio[k] * value
        out_ref[32 + k : 33 + k, :] = value * (1.0 / NX) * (1.0 / NY)


def backward_kernel(
    gx_ref, gy_ref, mu_ref, sines_ref, tc_ref, ts_ref, common_ref, first_ref, line_ref, carry_ref,
    in_ref, out_ref, p_ref, z_ref, grid_ref,
):
    eigen = eigen_table(sines_ref[...], mu_ref[pl.ds(gx_ref[0], 1), :], True)
    rho, gap, factor = decay(eigen)
    at_zero = jnp.logical_and(iota((32, 128), 0) == 0, iota((32, 128), 1) == 0)
    factor = factor * jnp.where(at_zero, 1.0 / NX, 2.0 / NX)
    south = carry_ref[pl.ds(0, 32, stride=8), :]
    north = carry_ref[pl.ds(1, 32, stride=8), :]

    def from_south(j, c):
        c = c - gap * c
        p_ref[pl.ds(j, 32, stride=ROWS), :] = in_ref[pl.ds(j, 32, stride=ROWS), :] + c
        return c

    c = lax.fori_loop(0, 128, from_south, south, unroll=8)
    c = c - gap * c
    p_ref[pl.ds(128, 32, stride=ROWS), :] = (in_ref[pl.ds(128, 32, stride=ROWS), :] + c + north) * factor

    def from_north(n, h):
        j = 127 - n
        h = h - gap * h
        p_ref[pl.ds(j, 32, stride=ROWS), :] = (p_ref[pl.ds(j, 32, stride=ROWS), :] + h) * factor
        return h

    lax.fori_loop(0, 128, from_north, north, unroll=8)
    for r in range(129, ROWS):
        p_ref[pl.ds(r, 32, stride=ROWS), :] = jnp.zeros((32, 128), f32)

    own = gy_ref[0]
    line = line_ref[pl.ds(own, 1), :] * (1.0 / NX)
    after = line_ref[pl.ds((own + 1) % 32, 1), :] * (1.0 / NX)
    lane128 = iota((128, 128), 1)
    column = jnp.where(iota((128, 128), 0) == 0, line, 0.0).T
    p_ref[0:128, :] = jnp.where(lane128 == 0, column, p_ref[0:128, :])
    lane1 = iota((1, 128), 1)
    p_ref[128:129, :] = jnp.where(lane1 == 0, after, p_ref[128:129, :])

    z_ref[0] = jnp.dot(p_ref[0:ROWS, :], first_ref[...], precision=highest, preferred_element_type=f32)

    def product(c, carry):
        start = pl.multiple_of(c * ROWS, 8)
        z_ref[c] = jnp.dot(
            p_ref[pl.ds(start, ROWS), :], common_ref[...], precision=highest, preferred_element_type=f32
        )
        return carry

    lax.fori_loop(1, 32, product, 0)

    def group(i, carry):
        start = pl.multiple_of(i * 8, 8)
        rows = pl.ds(start, 8)
        h = [(z_ref[0, rows, 0:128], z_ref[0, rows, 128:256])]
        for c in range(1, 32):
            re, im = z_ref[c, rows, 0:128], z_ref[c, rows, 128:256]
            tc, ts = tc_ref[c : c + 1, :], ts_ref[c : c + 1, :]
            h.append((re * tc - im * ts, im * tc + re * ts))
        x = backward_classes(h)
        for g in range(32):
            grid_ref[g, rows, :] = x[g]
        return carry

    lax.fori_loop(0, ROWS // 8, group, 0)

    for s in range(8):
        for part in range(4):
            tile = grid_ref[4 * s + part, 0:128, :].T
            out_ref[s, 128 * part : 128 * part + 128, :] = tile
            if part == 0 and s > 0:
                out_ref[s - 1, 512:513, :] = tile[0:1]
            out_ref[s, 513 + part : 514 + part, :] = grid_ref[4 * s + part, 128:129, :]
        out_ref[s, 517:520, :] = jnp.zeros((3, 128), f32)
    out_ref[7, 512:513, :] = jnp.zeros((1, 128), f32)


def gradient_kernel(
    gx_ref, thick_ref, unmix_ref, line_ref, p_ref, u_ref, v_ref, w_ref, uo_ref, vo_ref, wo_ref, press_ref, edge_ref
):
    step = pl.program_id(0)
    base = pl.multiple_of(step * 128, 128)
    wall = jnp.logical_and(gx_ref[0] == 7, step == 3)
    edge_ref[...] = jnp.zeros((128, 128), f32)
    for k in range(8):
        acc = p_ref[0, pl.ds(513 + step, 1), :] * unmix_ref[8 * k : 8 * k + 1, :]
        for mode in range(1, 8):
            acc = acc + p_ref[mode, pl.ds(513 + step, 1), :] * unmix_ref[8 * k + mode : 8 * k + mode + 1, :]
        edge_ref[k : k + 1, :] = acc
    edge_ref[...] = edge_ref[...].T
    for sub in range(17):
        parts = [p_ref[mode, pl.ds(base + 8 * sub, 8), :] for mode in range(8)]
        for k in range(8):
            acc = parts[0] * unmix_ref[8 * k : 8 * k + 1, :]
            for mode in range(1, 8):
                acc = acc + parts[mode] * unmix_ref[8 * k + mode : 8 * k + mode + 1, :]
            press_ref[k, 8 * sub : 8 * sub + 8, :] = acc
    lane = iota((16, 128), 1)
    row = iota((16, 128), 0)
    ones = jnp.ones((1, 128), f32)
    t = [ones * thick_ref[k] for k in range(8)]
    inverse = [2.0 / (t[k] + t[k + 1]) for k in range(7)]
    drift = [(line_ref[33 + k : 34 + k, :] - line_ref[32 + k : 33 + k, :]) * inverse[k] for k in range(7)]
    for sub in range(8):
        rows = slice(16 * sub, 16 * sub + 16)
        edge = edge_ref[rows, :]
        for k in range(8):
            p = press_ref[k, rows, :]
            east = press_ref[k, 16 * sub + 1 : 16 * sub + 17, :]
            u = u_ref[k, rows, :] - (east - p)
            if sub == 7:
                u = jnp.where(jnp.logical_and(wall, row == 15), 0.0, u)
            uo_ref[k, rows, :] = u
            north = jnp.where(lane == 127, pltpu.roll(edge, 127 - k, axis=1), pltpu.roll(p, 127, axis=1))
            vo_ref[k, rows, :] = v_ref[k, rows, :] - (north - p)
            if k < 7:
                wo_ref[k, rows, :] = w_ref[k, rows, :] - ((press_ref[k + 1, rows, :] - p) * inverse[k] + drift[k])
            else:
                wo_ref[k, rows, :] = jnp.zeros((16, 128), f32)


SMEM = pl.BlockSpec(memory_space=pltpu.SMEM)
VMEM = pl.BlockSpec(memory_space=pltpu.VMEM)


def whole(shape):
    return pl.BlockSpec(shape, lambda i: (0,) * len(shape))


def on_device(u_vel, v_vel, w_vel, thickness):
    gx = lax.axis_index("gx").astype(jnp.int32)[None]
    gy = lax.axis_index("gy").astype(jnp.int32)[None]
    common, first, tc, ts = dct_tables()
    sines = const(np.sin(math.pi * class_modes() / 8192) ** 2)
    tables = (sines, const(tc), const(ts))
    shape = jax.ShapeDtypeStruct

    mix, unmix, mu = pl.pallas_call(
        vertical_modes,
        out_shape=(shape((64, 128), f32), shape((64, 128), f32), shape((8, 128), f32)),
        in_specs=[SMEM],
        out_specs=(VMEM, VMEM, VMEM),
        name="vertical_modes",
    )(thickness)

    block = pl.BlockSpec((8, 128, 128), lambda i: (0, i, 0))
    field = (8, PAY, 128)
    packed = pl.pallas_call(
        divergence_kernel,
        out_shape=shape(field, f32),
        grid=(4,),
        in_specs=[SMEM, SMEM, whole((64, 128)), block, block, block],
        out_specs=whole(field),
        scratch_shapes=[pltpu.VMEM((64, 128), f32), pltpu.VMEM((64, 128), f32)],
        name="divergence",
    )(gx, thickness, mix, u_vel, v_vel, w_vel)
    packed = lax.all_to_all(packed, "gx", split_axis=0, concat_axis=0, tiled=True)

    local, small = pl.pallas_call(
        forward_kernel,
        out_shape=(shape((32 * ROWS, 128), f32), shape((256, 128), f32)),
        in_specs=[SMEM] + [VMEM] * 7,
        out_specs=(VMEM, VMEM),
        scratch_shapes=[
            pltpu.VMEM((32, ROWS, 128), f32),
            pltpu.VMEM((32, ROWS, 256), f32),
            pltpu.VMEM((32 * ROWS, 128), f32),
        ],
        name="forward",
    )(gx, mu, *tables, const(common), const(first), packed)
    small = lax.all_to_all(small, "gy", split_axis=0, concat_axis=0, tiled=True)

    carries = pl.pallas_call(
        carry_kernel,
        out_shape=shape((256, 128), f32),
        in_specs=[SMEM, SMEM] + [VMEM] * 3,
        out_specs=VMEM,
        name="carries",
    )(gx, gy, mu, sines, small)
    carries = lax.all_to_all(carries, "gy", split_axis=0, concat_axis=0, tiled=True)
    line = pl.pallas_call(
        line_kernel,
        out_shape=shape((40, 128), f32),
        in_specs=[SMEM, SMEM] + [VMEM] * 9,
        out_specs=VMEM,
        name="line",
    )(gx, thickness, mu, *[const(x) for x in line_tables()], small)

    packed = pl.pallas_call(
        backward_kernel,
        out_shape=shape(field, f32),
        in_specs=[SMEM, SMEM] + [VMEM] * 9,
        out_specs=VMEM,
        scratch_shapes=[
            pltpu.VMEM((32 * ROWS, 128), f32),
            pltpu.VMEM((32, ROWS, 256), f32),
            pltpu.VMEM((32, ROWS, 128), f32),
        ],
        name="backward",
    )(gx, gy, mu, *tables, const(common.T), const(first.T), line, carries, local)
    packed = lax.all_to_all(packed, "gx", split_axis=0, concat_axis=0, tiled=True)

    out = shape((8, LX, 128), f32)
    return pl.pallas_call(
        gradient_kernel,
        out_shape=(out, out, out),
        grid=(4,),
        in_specs=[SMEM, SMEM, whole((64, 128)), whole((40, 128)), whole(field), block, block, block],
        out_specs=(block, block, block),
        scratch_shapes=[pltpu.VMEM((8, 136, 128), f32), pltpu.VMEM((128, 128), f32)],
        name="gradient",
    )(gx, thickness, unmix, line, packed, u_vel, v_vel, w_vel)


def solution(mesh):
    return jax.shard_map(
        on_device,
        mesh=mesh,
        in_specs=(P(None, "gx", "gy"), P(None, "gx", "gy"), P(None, "gx", "gy"), P()),
        out_specs=(P(None, "gx", "gy"), P(None, "gx", "gy"), P(None, "gx", "gy")),
        check_vma=False,
    )
```

```python
import math

import jax
import jax.numpy as jnp
import numpy as np
from jax import lax
from jax.experimental import pallas as pl
from jax.experimental.pallas import tpu as pltpu
from jax.sharding import PartitionSpec as P

highest = lax.Precision.HIGHEST
f32 = jnp.float32
NX = 4096
NY = 4096
NZ = 8
LX = 512
ROWS = 136
BATCH = 4
PAY = 520
HALF = float(np.sqrt(0.5))

CLASSES = [0] + [mu + 16 * tau for mu in range(1, 8) for tau in range(4)] + [16, 8, 24]


def class_modes():
    t = np.arange(64)
    rows = [np.concatenate([64 * t, 64 * t + 32])]
    for nu in CLASSES[1:]:
        rows.append(np.concatenate([64 * t + nu, 64 * (t + 1) - nu]))
    return np.stack(rows)


def dct_tables():
    b = np.arange(128)[:, None]
    t = np.arange(64)[None, :]
    near = math.pi * t * (2 * b + 1) / 128
    far = math.pi * (t + 1) * (2 * b + 1) / 128
    common = np.block([[np.cos(near), np.cos(far)], [np.sin(near), -np.sin(far)]])
    zero = np.zeros((128, 64))
    middle = np.cos(math.pi * (64 * t + 32) * (2 * b + 1) / 8192)
    first = np.block([[np.cos(near), zero], [zero, middle]])
    nu = np.array(CLASSES)[:, None]
    angle = math.pi * nu * (2 * np.arange(128)[None, :] + 1) / 8192
    return common, first, np.cos(angle), np.sin(angle)


def line_tables():
    d = np.arange(32)
    j = np.arange(128)
    a32 = 2 * math.pi * (d[:, None] * d[None, :] % 32) / 32
    a128 = 2 * math.pi * (j[:, None] * j[None, :] % 128) / 128
    tw = 2 * math.pi * (d[:, None] * j[None, :]) / 4096
    q = d[:, None] + 32 * j[None, :]
    lam = -4.0 * np.sin(math.pi * q / NY) ** 2
    return np.cos(a32), np.sin(a32), np.cos(tw), np.sin(tw), np.cos(a128), np.sin(a128), lam


def three_parts(values):
    rest = np.asarray(values, dtype=np.float32)
    parts = []
    for _ in range(3):
        part = rest.astype(jnp.bfloat16)
        parts.append(part)
        rest = rest - part.astype(np.float32)
    return parts


def forward_weights(matrix):
    high, mid, low = three_parts(matrix)
    return jnp.asarray(np.concatenate([high, mid, low, np.zeros_like(low)], axis=1))


def backward_weights(matrix):
    high, mid, low = three_parts(matrix.T)
    return jnp.asarray(np.concatenate([high, high, mid, mid, low, high], axis=0))


def head(x):
    scaled = x * 65537.0
    return scaled - (scaled - x)


def split(x):
    high = x.astype(jnp.bfloat16)
    rest = x - high.astype(f32)
    mid = head(rest)
    return high, mid.astype(jnp.bfloat16), (rest - mid).astype(jnp.bfloat16)


def times_bf16(a, b):
    return jnp.dot(a, b, preferred_element_type=f32)


def forward_product(x, w_ref):
    high, mid, low = split(x)
    both = times_bf16(high, w_ref[:, 0:256]) + times_bf16(mid, w_ref[:, 0:256])
    rest = times_bf16(high, w_ref[:, 256:384]) + times_bf16(low, w_ref[:, 0:128])
    return both[:, 0:128] + (both[:, 128:256] + rest)


def backward_product(x, w_ref):
    high, mid, low = split(x)
    two = jnp.concatenate([high, mid], axis=1)
    rest = times_bf16(two, w_ref[256:512, :]) + times_bf16(jnp.concatenate([high, low], axis=1), w_ref[512:768, :])
    return times_bf16(two, w_ref[0:256, :]) + rest


def slow_table():
    slow = class_modes()[:, [0, 1, 2, 3, 64, 65, 66, 67]].T
    return np.sin(math.pi * np.tile(slow, (1, 4)) / 8192) ** 2


def const(values):
    return jnp.asarray(np.asarray(values, dtype=np.float32))


def across_blocks(x):
    e = [x[s] + x[s + 4] for s in range(4)]
    o = [x[s] - x[s + 4] for s in range(4)]
    out = [None] * 9
    e02, e13 = e[0] + e[2], e[1] + e[3]
    out[0] = e02 + e13
    out[8] = e02 - e13
    out[4] = (e[0] - e[2], e[3] - e[1])
    d13, s13 = HALF * (o[1] - o[3]), HALF * (o[1] + o[3])
    out[2] = (o[0] + d13, -o[2] - s13)
    out[6] = (o[0] - d13, o[2] - s13)
    zr, zi = [x[0]], [-x[4]]
    for s in (1, 2, 3):
        c, q = math.cos(math.pi * s / 8), math.sin(math.pi * s / 8)
        zr.append(x[s] * c - x[s + 4] * q)
        zi.append(-(x[s] * q + x[s + 4] * c))
    y = four(zr, zi)
    out[1] = y[0]
    out[5] = y[1]
    out[7] = (y[2][0], -y[2][1])
    out[3] = (y[3][0], -y[3][1])
    return out


def four(zr, zi):
    t0r, t0i = zr[0] + zr[2], zi[0] + zi[2]
    t1r, t1i = zr[0] - zr[2], zi[0] - zi[2]
    t2r, t2i = zr[1] + zr[3], zi[1] + zi[3]
    t3r, t3i = zr[1] - zr[3], zi[1] - zi[3]
    return [
        (t0r + t2r, t0i + t2i),
        (t1r + t3i, t1i - t3r),
        (t0r - t2r, t0i - t2i),
        (t1r - t3i, t1i + t3r),
    ]


def four_back(h):
    zr = [v[0] for v in h]
    zi = [v[1] for v in h]
    t0r, t0i = zr[0] + zr[2], zi[0] + zi[2]
    t1r, t1i = zr[0] - zr[2], zi[0] - zi[2]
    t2r, t2i = zr[1] + zr[3], zi[1] + zi[3]
    t3r, t3i = zr[1] - zr[3], zi[1] - zi[3]
    return [
        (t0r + t2r, t0i + t2i),
        (t1r - t3i, t1i + t3r),
        (t0r - t2r, t0i - t2i),
        (t1r + t3i, t1i - t3r),
    ]


def forward_classes(x):
    per_a = [across_blocks([x[4 * s + a] for s in range(8)]) for a in range(4)]
    out = []
    y0 = [per_a[a][0] for a in range(4)]
    y8 = [per_a[a][8] for a in range(4)]
    out.append(((y0[0] + y0[2]) + (y0[1] + y0[3]), (y0[0] + y0[2]) - (y0[1] + y0[3])))
    for mu in range(1, 8):
        zr, zi = [per_a[0][mu][0]], [per_a[0][mu][1]]
        for a in (1, 2, 3):
            yr, yi = per_a[a][mu]
            c, q = math.cos(math.pi * mu * a / 32), math.sin(math.pi * mu * a / 32)
            zr.append(yr * c + yi * q)
            zi.append(yi * c - yr * q)
        out.extend(four(zr, zi))
    out.append((y0[0] - y0[2], y0[3] - y0[1]))
    d13, s13 = HALF * (y8[1] - y8[3]), HALF * (y8[1] + y8[3])
    out.append((y8[0] + d13, -y8[2] - s13))
    out.append((y8[0] - d13, y8[2] - s13))
    return out


def backward_classes(h):
    h0, h32 = h[0]
    h16, h8, h24 = h[29], h[30], h[31]
    x = [None] * 32
    by_mu = {}
    for mu in range(1, 8):
        z = four_back(h[1 + 4 * (mu - 1) : 5 + 4 * (mu - 1)])
        for a in (1, 2, 3):
            c, q = math.cos(math.pi * mu * a / 32), math.sin(math.pi * mu * a / 32)
            zr, zi = z[a]
            z[a] = (zr * c - zi * q, zr * q + zi * c)
        by_mu[mu] = z
    sum0, dif0 = h0 + h32, h0 - h32
    y0 = [sum0 + h16[0], dif0 - h16[1], sum0 - h16[0], dif0 + h16[1]]
    dr, di = HALF * (h8[0] - h24[0]), HALF * (h8[1] + h24[1])
    y8 = [h8[0] + h24[0], dr - di, h24[1] - h8[1], -dr - di]
    for a in range(4):
        y = {mu: by_mu[mu][a] for mu in by_mu}
        ea, eb = y0[a] + y8[a], y0[a] - y8[a]
        y2, y4, y6 = y[2], y[4], y[6]
        rep = [ea + y4[0], eb - y4[1], ea - y4[0], eb + y4[1]]
        er, ei = HALF * (y2[0] - y6[0]), HALF * (y2[1] + y6[1])
        alt = [y2[0] + y6[0], er - ei, y6[1] - y2[1], -er - ei]
        u = four_back([y[1], y[5], (y[7][0], -y[7][1]), (y[3][0], -y[3][1])])
        for s in range(4):
            ur, ui = u[s]
            if s:
                c, q = math.cos(math.pi * s / 8), math.sin(math.pi * s / 8)
                ur, ui = ur * c - ui * q, ur * q + ui * c
            x[4 * s + a] = rep[s] + alt[s] + ur
            x[4 * (s + 4) + a] = rep[s] - alt[s] - ui
    return x


def decay(eigen):
    half = 0.5 * jnp.sqrt(-eigen)
    root = jnp.sqrt(1.0 + half * half)
    gap = 2.0 * half * (root - half)
    return 1.0 - gap, gap, -0.25 / (half * root)


def doubled(gap, times):
    for _ in range(times):
        gap = gap * (2.0 - gap)
    return gap


ROUNDS = []
_seats = list(range(8))
for _ in range(7):
    ROUNDS.append([tuple(sorted((_seats[i], _seats[7 - i]))) for i in range(4)])
    _seats = [_seats[0], _seats[7]] + _seats[1:7]
SWEEPS = 6
PAIRS = [(i, j) for i in range(8) for j in range(i, 8)]


def vertical_modes(thick_ref, mix_ref, unmix_ref, mu_ref):
    t = [jnp.full((8, 128), thick_ref[k], f32) for k in range(8)]
    unit = 16384.0
    zero = jnp.zeros((8, 128), f32)
    one = jnp.ones((8, 128), f32)
    centre = [0.5 * (t[k] + t[k + 1]) for k in range(7)]
    root = [jnp.sqrt(t[k]) for k in range(8)]
    a = {pair: zero for pair in PAIRS}
    for k in range(8):
        total = zero
        if k < 7:
            total = total + unit / (t[k] * centre[k])
            a[(k, k + 1)] = unit / (centre[k] * (root[k] * root[k + 1]))
        if k > 0:
            total = total + unit / (t[k] * centre[k - 1])
        a[(k, k)] = -total
    vec = [[one if i == j else zero for j in range(8)] for i in range(8)]

    def sweep(_, carry):
        flat_a, flat_v = carry
        a = dict(zip(PAIRS, flat_a))
        vec = [list(flat_v[8 * i : 8 * i + 8]) for i in range(8)]

        def get(i, j):
            return a[(i, j) if i <= j else (j, i)]

        for pairs in ROUNDS:
            turn = {}
            for p, q in pairs:
                off = a[(p, q)]
                diff = a[(q, q)] - a[(p, p)]
                size = jnp.sqrt(diff * diff + 4.0 * off * off)
                low = jnp.where(diff < 0.0, diff - size, diff + size)
                tan = 2.0 * off / jnp.where(low == 0.0, 1.0, low)
                cos = 1.0 / jnp.sqrt(1.0 + tan * tan)
                turn[(p, q)] = (cos, tan * cos, tan)
            full = [[get(i, j) for j in range(8)] for i in range(8)]
            for p, q in pairs:
                cos, sin, _t = turn[(p, q)]
                for i in range(8):
                    x, y = full[i][p], full[i][q]
                    full[i][p], full[i][q] = cos * x - sin * y, sin * x + cos * y
                    x, y = vec[i][p], vec[i][q]
                    vec[i][p], vec[i][q] = cos * x - sin * y, sin * x + cos * y
            for p, q in pairs:
                cos, sin, tan = turn[(p, q)]
                for j in range(8):
                    x, y = full[p][j], full[q][j]
                    full[p][j], full[q][j] = cos * x - sin * y, sin * x + cos * y
            diag = {}
            for p, q in pairs:
                cos, sin, tan = turn[(p, q)]
                off = a[(p, q)]
                diag[p] = a[(p, p)] - tan * off
                diag[q] = a[(q, q)] + tan * off
            a = {(i, j): full[i][j] for i, j in PAIRS}
            for p, q in pairs:
                a[(p, q)] = zero
            for p in diag:
                a[(p, p)] = diag[p]
        return tuple(a[pair] for pair in PAIRS), tuple(vec[i][j] for i in range(8) for j in range(8))

    start = (tuple(a[pair] for pair in PAIRS), tuple(vec[i][j] for i in range(8) for j in range(8)))
    flat_a, flat_v = lax.fori_loop(0, SWEEPS, sweep, start)
    a = dict(zip(PAIRS, flat_a))
    for mode in range(8):
        mu_ref[mode : mode + 1, :] = jnp.minimum(a[(mode, mode)] * (1.0 / unit), 0.0)[0:1]
        for k in range(8):
            entry = flat_v[8 * k + mode]
            mix_ref[8 * mode + k : 8 * mode + k + 1, :] = (entry * root[k])[0:1]
            unmix_ref[8 * k + mode : 8 * k + mode + 1, :] = (entry / root[k])[0:1]


def iota(shape, axis):
    return lax.broadcasted_iota(jnp.int32, shape, axis)


def divergence_kernel(
    gx_ref, thick_ref, u_hbm, v_hbm, w_hbm, out_ref, unmix_ref, mu_ref,
    mix_ref, u_ref, v_ref, w_ref, last_ref, sum_ref, sems,
):
    def copies(step):
        rows = pl.ds(128 * step, 128)
        return [
            pltpu.make_async_copy(src.at[:, rows, :], dst.at[:, rows, :], sems.at[n, step])
            for n, (src, dst) in enumerate(((u_hbm, u_ref), (v_hbm, v_ref), (w_hbm, w_ref)))
        ]

    for step in range(4):
        for copy in copies(step):
            copy.start()
    vertical_modes(thick_ref, mix_ref, unmix_ref, mu_ref)

    last_ref[...] = jnp.zeros((64, 128), f32)
    sum_ref[...] = jnp.zeros((64, 128), f32)
    lane = iota((16, 128), 1)
    row = iota((16, 128), 0)
    lanes = iota((128, 128), 1)
    ones = jnp.ones((1, 128), f32)
    inverse = [1.0 / (ones * thick_ref[k]) for k in range(8)]

    def block(step, carry):
        for copy in copies(step):
            copy.wait()
        wall = jnp.logical_and(gx_ref[0] == 7, step == 3)
        base = pl.multiple_of(step * 128, 128)
        for sub in range(8):
            rows = pl.ds(base + 16 * sub, 16)
            div = []
            below = None
            for k in range(8):
                u = u_ref[k, rows, :]
                if sub == 7:
                    u = jnp.where(jnp.logical_and(wall, row == 15), 0.0, u)
                prev = pltpu.roll(u, 1, axis=0)
                prev = jnp.where(row == 0, last_ref[8 * k : 8 * k + 1, :], prev)
                last_ref[8 * k : 8 * k + 1, :] = u[15:16]
                v = v_ref[k, rows, :]
                back = jnp.where(lane == 0, 0.0, pltpu.roll(v, 1, axis=1))
                if k < 7:
                    w = w_ref[k, rows, :]
                    up = w if below is None else w - below
                    below = w
                else:
                    up = -below
                rise = up * inverse[k]
                sum_ref[8 * k : 8 * k + 8, :] += rise[0:8] + rise[8:16]
                div.append((u - prev) + (v - back) + rise)
            for mode in range(8):
                acc = div[0] * mix_ref[8 * mode : 8 * mode + 1, :]
                for k in range(1, 8):
                    acc = acc + div[k] * mix_ref[8 * mode + k : 8 * mode + k + 1, :]
                out_ref[mode, rows, :] = acc

        edge = jnp.zeros((128, 128), f32)
        for k in range(8):
            edge = jnp.where(lanes == k, pltpu.roll(v_ref[k, pl.ds(base, 128), :], k + 1, axis=1), edge)
        edge = edge.T
        for mode in range(8):
            acc = edge[0:1] * mix_ref[8 * mode : 8 * mode + 1, :]
            for k in range(1, 8):
                acc = acc + edge[k : k + 1] * mix_ref[8 * mode + k : 8 * mode + k + 1, :]
            out_ref[mode, pl.ds(513 + step, 1), :] = -acc
        return carry

    lax.fori_loop(0, 4, block, 0)

    lane1 = iota((1, 128), 1)
    totals = jnp.zeros((1, 128), f32)
    for k in range(8):
        part = jnp.sum(sum_ref[8 * k : 8 * k + 8, :], axis=0, keepdims=True)
        part = jnp.sum(part, axis=1, keepdims=True)
        totals = jnp.where(lane1 == k, part, totals)
    for mode in range(8):
        acc = last_ref[0:1, :] * mix_ref[8 * mode : 8 * mode + 1, :]
        for k in range(1, 8):
            acc = acc + last_ref[8 * k : 8 * k + 1, :] * mix_ref[8 * mode + k : 8 * mode + k + 1, :]
        out_ref[mode, 512:513, :] = acc
        out_ref[mode, 517:518, :] = totals
        out_ref[mode, 518:520, :] = jnp.zeros((2, 128), f32)


def eigen_table(sines, mu_row, with_first):
    eigen = mu_row - 4.0 * sines
    if with_first:
        first = jnp.logical_and(iota(sines.shape, 0) == 0, iota(sines.shape, 1) == 0)
        eigen = jnp.where(first, -1.0, eigen)
    return eigen


def forward_kernel(
    gx_ref, mu_ref, sines_ref, tc_ref, ts_ref, common_ref, first_ref, in_ref, out_ref, small_ref,
    south_ref, north_ref, grid_ref, y_ref, side_ref, turn_ref,
):
    row8 = iota((8, 128), 0)
    row128 = iota((128, 128), 0)
    for s in range(8):
        for part in range(4):
            tile = in_ref[s, 128 * part : 128 * part + 128, :]
            if part == 0 and s > 0:
                tile = jnp.where(row128 == 0, tile - in_ref[s - 1, 512:513, :], tile)
            grid_ref[4 * s + part, 0:128, :] = tile.T
            ghost = in_ref[s, 513 + part : 514 + part, :]
            grid_ref[4 * s + part, 128:136, :] = jnp.where(row8 == 0, ghost, 0.0)

    def group(i, carry):
        start = pl.multiple_of(i * 8, 8)
        y = forward_classes([grid_ref[g, pl.ds(start, 8), :] for g in range(32)])
        y_ref[pl.ds(start, 8), 0:128] = y[0][0]
        y_ref[pl.ds(start, 8), 128:256] = y[0][1]
        for c in range(1, 32):
            re, im = y[c]
            tc, ts = tc_ref[c : c + 1, :], ts_ref[c : c + 1, :]
            rows = pl.ds(start + ROWS * c, 8)
            y_ref[rows, 0:128] = re * tc + im * ts
            y_ref[rows, 128:256] = im * tc - re * ts
        return carry

    lax.fori_loop(0, ROWS // 8, group, 0)

    batch = BATCH * ROWS

    def product(n, carry):
        start = pl.multiple_of(n * batch, 8)
        out_ref[pl.ds(start, batch), :] = forward_product(y_ref[pl.ds(start, batch), :], common_ref)
        return carry

    lax.fori_loop(0, 32 // BATCH, product, 0)
    out_ref[0:144, :] = jnp.where(
        iota((144, 128), 0) < ROWS, forward_product(y_ref[0:144, :], first_ref), out_ref[0:144, :]
    )

    line = out_ref[0:128, :].T[0:1]
    ghost_line = out_ref[128:129, :]

    eigen = eigen_table(sines_ref[...], mu_ref[pl.ds(gx_ref[0], 1), :], True)
    rho, gap, _ = decay(eigen)
    ghost = out_ref[pl.ds(128, 32, stride=ROWS), :]

    def from_north(n, b):
        j = 127 - n
        side_ref[pl.ds(j, 32, stride=ROWS), :] = rho * b
        return out_ref[pl.ds(j, 32, stride=ROWS), :] + (b - gap * b)

    b = lax.fori_loop(0, 128, from_north, ghost, unroll=8)

    def from_south(j, f):
        f = out_ref[pl.ds(j, 32, stride=ROWS), :] + (f - gap * f)
        out_ref[pl.ds(j, 32, stride=ROWS), :] = f + side_ref[pl.ds(j, 32, stride=ROWS), :]
        return f

    f = lax.fori_loop(0, 128, from_south, jnp.zeros((32, 128), f32), unroll=8)
    out_ref[pl.ds(128, 32, stride=ROWS), :] = rho * f + ghost

    totals = in_ref[0, 517:518, :]
    for s in range(1, 8):
        totals = totals + in_ref[s, 517:518, :]
    f = f + ghost / rho
    south_ref[...] = f
    north_ref[...] = b
    turn_ref[0:32, :] = f
    turn_ref[32:64, :] = b
    turn_ref[64:128, :] = jnp.zeros((64, 128), f32)
    turn_ref[...] = turn_ref[...].T
    turn_ref[4:8, :] = turn_ref[64:68, :]
    lane1 = iota((1, 128), 1)
    extra = [pltpu.roll(line, 64, axis=1), line, pltpu.roll(totals, 64, axis=1), pltpu.roll(ghost_line, 64, axis=1)]
    for r in range(4):
        turn_ref[r : r + 1, :] = jnp.where(lane1 < 64, turn_ref[r : r + 1, :], extra[r])
    for d in range(32):
        small_ref[8 * d : 8 * d + 8, :] = turn_ref[0:8, :]


def line_kernel(
    gx_ref, gy_ref, thick_ref, mu_ref, slow_ref, c32_ref, s32_ref, tc_ref, ts_ref, c128_ref, s128_ref, lam_ref,
    in_ref, out_ref, turn_ref,
):
    def times(a, b):
        return jnp.dot(a, b, precision=highest, preferred_element_type=f32)

    own = gy_ref[0]
    eigen = mu_ref[pl.ds(gx_ref[0], 1), :] - 4.0 * slow_ref[...]
    lane8 = iota((8, 128), 1)
    first = jnp.logical_and(iota((8, 128), 0) == 0, lane8 % 32 == 0)
    _, gap, _ = decay(jnp.where(first, -1.0, eigen))
    gap_block = doubled(gap, 7)
    around = 1.0 / doubled(gap_block, 5)
    c = jnp.zeros((8, 128), f32)
    h = jnp.zeros((8, 128), f32)
    for e in range(32, 0, -1):
        c = in_ref[pl.ds(pl.multiple_of((own + 32 - e) % 32 * 8, 8), 8), :] + (c - gap_block * c)
        h = in_ref[pl.ds(pl.multiple_of((own + e) % 32 * 8, 8), 8), :] + (h - gap_block * h)
    carry = jnp.where(lane8 < 32, c, h) * around
    turn_ref[...] = jnp.zeros((128, 128), f32)
    turn_ref[0:4, :] = carry[0:4]
    turn_ref[64:68, :] = carry[4:8]
    out_ref[40:104, :] = turn_ref[...].T[0:64]

    lane32 = iota((32, 128), 1)
    line = jnp.where(
        lane32 < 64,
        pltpu.roll(in_ref[pl.ds(0, 32, stride=8), :], 64, axis=1),
        in_ref[pl.ds(1, 32, stride=8), :],
    )
    ghost = pltpu.roll(in_ref[pl.ds(3, 32, stride=8), :], 64, axis=1)
    at_first = iota((32, 128), 1) == 0
    line = line + jnp.where(at_first, pltpu.roll(ghost, 1, axis=0), 0.0)
    c32, s32 = c32_ref[...], s32_ref[...]
    tc, ts = tc_ref[...], ts_ref[...]
    c128, s128 = c128_ref[...], s128_ref[...]
    re, im = times(c32, line), -times(s32, line)
    re, im = re * tc + im * ts, im * tc - re * ts
    re, im = times(re, c128) + times(im, s128), times(im, c128) - times(re, s128)
    mean = jnp.logical_and(iota((32, 128), 0) == 0, at_first)
    eigen = mu_ref[pl.ds(gx_ref[0], 1), :] + lam_ref[...]
    gain = jnp.where(mean, 0.0, (1.0 / NY) / jnp.where(mean, 1.0, eigen))
    re, im = re * gain, im * gain
    re, im = times(re, c128) - times(im, s128), times(im, c128) + times(re, s128)
    re, im = re * tc - im * ts, im * tc + re * ts
    out_ref[0:32, :] = times(c32, re) - times(s32, im)

    totals = jnp.sum(in_ref[pl.ds(2, 32, stride=8), :], axis=0, keepdims=True)
    totals = pltpu.roll(totals, 64, axis=1)
    lane = iota((1, 128), 1)
    ones = jnp.ones((1, 128), f32)
    rhs = [ones * jnp.sum(jnp.where(lane == k, totals, 0.0), axis=1, keepdims=True) for k in range(8)]
    t = [ones * thick_ref[k] for k in range(8)]
    centre = [0.5 * (t[k] + t[k + 1]) for k in range(7)]
    zero = jnp.zeros((1, 128), f32)
    upper = [1.0 / (t[k] * centre[k]) for k in range(7)] + [zero]
    lower = [zero] + [1.0 / (t[k] * centre[k - 1]) for k in range(1, 8)]
    reduced, ratio = [], []
    excess = zero
    for k in range(8):
        if k == 0:
            excess = -upper[0]
            top = rhs[0]
        else:
            excess = lower[k] * excess / (upper[k - 1] - excess)
            top = rhs[k] - lower[k] * reduced[-1]
        pivot = excess - upper[k]
        reduced.append(top / pivot)
        ratio.append(upper[k] / pivot)
    value = zero
    for k in reversed(range(8)):
        value = reduced[k] - ratio[k] * value
        out_ref[32 + k : 33 + k, :] = value * (1.0 / NX) * (1.0 / NY)


def backward_kernel(
    gx_ref, gy_ref, mu_ref, sines_ref, tc_ref, ts_ref, common_ref, first_ref, line_ref, south_ref,
    north_ref, in_ref, out_ref, p_ref, z_ref, grid_ref,
):
    eigen = eigen_table(sines_ref[...], mu_ref[pl.ds(gx_ref[0], 1), :], True)
    rho, gap, factor = decay(eigen)
    at_zero = jnp.logical_and(iota((32, 128), 0) == 0, iota((32, 128), 1) == 0)
    factor = factor * jnp.where(at_zero, 1.0 / NX, 2.0 / NX)
    slow = iota((32, 128), 1) % 64 < 4
    south = jnp.where(slow, line_ref[40:72, :], south_ref[...])
    north = jnp.where(slow, line_ref[72:104, :], north_ref[...])

    def from_south(j, c):
        c = c - gap * c
        p_ref[pl.ds(j, 32, stride=ROWS), :] = in_ref[pl.ds(j, 32, stride=ROWS), :] + c
        return c

    c = lax.fori_loop(0, 128, from_south, south, unroll=8)
    c = c - gap * c
    p_ref[pl.ds(128, 32, stride=ROWS), :] = (in_ref[pl.ds(128, 32, stride=ROWS), :] + c + north) * factor

    def from_north(n, h):
        j = 127 - n
        h = h - gap * h
        p_ref[pl.ds(j, 32, stride=ROWS), :] = (p_ref[pl.ds(j, 32, stride=ROWS), :] + h) * factor
        return h

    lax.fori_loop(0, 128, from_north, north, unroll=8)
    for r in range(129, ROWS):
        p_ref[pl.ds(r, 32, stride=ROWS), :] = jnp.zeros((32, 128), f32)

    own = gy_ref[0]
    line = line_ref[pl.ds(own, 1), :] * (1.0 / NX)
    after = line_ref[pl.ds((own + 1) % 32, 1), :] * (1.0 / NX)
    lane128 = iota((128, 128), 1)
    column = jnp.where(iota((128, 128), 0) == 0, line, 0.0).T
    p_ref[0:128, :] = jnp.where(lane128 == 0, column, p_ref[0:128, :])
    lane1 = iota((1, 128), 1)
    p_ref[128:129, :] = jnp.where(lane1 == 0, after, p_ref[128:129, :])

    batch = BATCH * ROWS

    def product(n, carry):
        start = pl.multiple_of(n * batch, 8)
        z_ref[pl.ds(start, batch), :] = backward_product(p_ref[pl.ds(start, batch), :], common_ref)
        return carry

    lax.fori_loop(0, 32 // BATCH, product, 0)
    z_ref[0:ROWS, :] = backward_product(p_ref[0:144, :], first_ref)[0:ROWS]

    def group(i, carry):
        start = pl.multiple_of(i * 8, 8)
        rows = pl.ds(start, 8)
        h = [(z_ref[rows, 0:128], z_ref[rows, 128:256])]
        for c in range(1, 32):
            part = pl.ds(start + ROWS * c, 8)
            re, im = z_ref[part, 0:128], z_ref[part, 128:256]
            tc, ts = tc_ref[c : c + 1, :], ts_ref[c : c + 1, :]
            h.append((re * tc - im * ts, im * tc + re * ts))
        x = backward_classes(h)
        for g in range(32):
            grid_ref[g, rows, :] = x[g]
        return carry

    lax.fori_loop(0, ROWS // 8, group, 0)

    for s in range(8):
        for part in range(4):
            tile = grid_ref[4 * s + part, 0:128, :].T
            out_ref[s, 128 * part : 128 * part + 128, :] = tile
            if part == 0 and s > 0:
                out_ref[s - 1, 512:513, :] = tile[0:1]
            out_ref[s, 513 + part : 514 + part, :] = grid_ref[4 * s + part, 128:129, :]
        out_ref[s, 517:520, :] = jnp.zeros((3, 128), f32)
    out_ref[7, 512:513, :] = jnp.zeros((1, 128), f32)


def gradient_kernel(
    gx_ref, thick_ref, unmix_ref, line_ref, p_ref, u_ref, v_ref, w_ref, uo_ref, vo_ref, wo_ref, press_ref, edge_ref
):
    step = pl.program_id(0)
    base = pl.multiple_of(step * 128, 128)
    wall = jnp.logical_and(gx_ref[0] == 7, step == 3)
    edge_ref[...] = jnp.zeros((128, 128), f32)
    for k in range(8):
        acc = p_ref[0, pl.ds(513 + step, 1), :] * unmix_ref[8 * k : 8 * k + 1, :]
        for mode in range(1, 8):
            acc = acc + p_ref[mode, pl.ds(513 + step, 1), :] * unmix_ref[8 * k + mode : 8 * k + mode + 1, :]
        edge_ref[k : k + 1, :] = acc
    edge_ref[...] = edge_ref[...].T
    for sub in range(17):
        parts = [p_ref[mode, pl.ds(base + 8 * sub, 8), :] for mode in range(8)]
        for k in range(8):
            acc = parts[0] * unmix_ref[8 * k : 8 * k + 1, :]
            for mode in range(1, 8):
                acc = acc + parts[mode] * unmix_ref[8 * k + mode : 8 * k + mode + 1, :]
            press_ref[k, 8 * sub : 8 * sub + 8, :] = acc
    lane = iota((16, 128), 1)
    row = iota((16, 128), 0)
    ones = jnp.ones((1, 128), f32)
    t = [ones * thick_ref[k] for k in range(8)]
    inverse = [2.0 / (t[k] + t[k + 1]) for k in range(7)]
    drift = [(line_ref[33 + k : 34 + k, :] - line_ref[32 + k : 33 + k, :]) * inverse[k] for k in range(7)]
    for sub in range(8):
        rows = slice(16 * sub, 16 * sub + 16)
        edge = edge_ref[rows, :]
        for k in range(8):
            p = press_ref[k, rows, :]
            east = press_ref[k, 16 * sub + 1 : 16 * sub + 17, :]
            u = u_ref[k, rows, :] - (east - p)
            if sub == 7:
                u = jnp.where(jnp.logical_and(wall, row == 15), 0.0, u)
            uo_ref[k, rows, :] = u
            north = jnp.where(lane == 127, pltpu.roll(edge, 127 - k, axis=1), pltpu.roll(p, 127, axis=1))
            vo_ref[k, rows, :] = v_ref[k, rows, :] - (north - p)
            if k < 7:
                wo_ref[k, rows, :] = w_ref[k, rows, :] - ((press_ref[k + 1, rows, :] - p) * inverse[k] + drift[k])
            else:
                wo_ref[k, rows, :] = jnp.zeros((16, 128), f32)


SMEM = pl.BlockSpec(memory_space=pltpu.SMEM)
VMEM = pl.BlockSpec(memory_space=pltpu.VMEM)


def params(mib):
    return pltpu.CompilerParams(vmem_limit_bytes=mib * 2**20)


def whole(shape):
    return pl.BlockSpec(shape, lambda i: (0,) * len(shape))


def on_device(u_vel, v_vel, w_vel, thickness):
    gx = lax.axis_index("gx").astype(jnp.int32)[None]
    gy = lax.axis_index("gy").astype(jnp.int32)[None]
    common, first, tc, ts = dct_tables()
    sines = const(np.sin(math.pi * class_modes() / 8192) ** 2)
    tables = (sines, const(tc), const(ts))
    shape = jax.ShapeDtypeStruct

    block = pl.BlockSpec((8, 128, 128), lambda i: (0, i, 0))
    field = (8, PAY, 128)
    local_field = pltpu.VMEM((8, LX, 128), f32)
    packed, unmix, mu = pl.pallas_call(
        divergence_kernel,
        out_shape=(shape(field, f32), shape((64, 128), f32), shape((8, 128), f32)),
        in_specs=[SMEM, SMEM] + [pl.BlockSpec(memory_space=pltpu.HBM)] * 3,
        out_specs=(VMEM, VMEM, VMEM),
        scratch_shapes=[
            pltpu.VMEM((64, 128), f32),
            local_field,
            local_field,
            local_field,
            pltpu.VMEM((64, 128), f32),
            pltpu.VMEM((64, 128), f32),
            pltpu.SemaphoreType.DMA((3, 4)),
        ],
        compiler_params=params(12),
        name="divergence",
    )(gx, thickness, u_vel, v_vel, w_vel)
    packed = lax.all_to_all(packed, "gx", split_axis=0, concat_axis=0, tiled=True)

    rows = shape((32, 128), f32)
    local, small, south, north = pl.pallas_call(
        forward_kernel,
        out_shape=(shape((32 * ROWS, 128), f32), shape((256, 128), f32), rows, rows),
        in_specs=[SMEM] + [VMEM] * 7,
        out_specs=(VMEM, VMEM, VMEM, VMEM),
        scratch_shapes=[
            pltpu.VMEM((32, ROWS, 128), f32),
            pltpu.VMEM((32 * ROWS, 256), f32),
            pltpu.VMEM((32 * ROWS, 128), f32),
            pltpu.VMEM((128, 128), f32),
        ],
        compiler_params=params(20),
        name="forward",
    )(gx, mu, *tables, forward_weights(common), forward_weights(first), packed)
    small = lax.all_to_all(small, "gy", split_axis=0, concat_axis=0, tiled=True)

    parts = lax.axis_size("gy")
    south = lax.ppermute(south, "gy", [(i, (i + 1) % parts) for i in range(parts)])
    north = lax.ppermute(north, "gy", [(i, (i - 1) % parts) for i in range(parts)])
    line = pl.pallas_call(
        line_kernel,
        out_shape=shape((104, 128), f32),
        in_specs=[SMEM, SMEM, SMEM] + [VMEM] * 10,
        out_specs=VMEM,
        scratch_shapes=[pltpu.VMEM((128, 128), f32)],
        compiler_params=params(4),
        name="line",
    )(gx, gy, thickness, mu, const(slow_table()), *[const(x) for x in line_tables()], small)

    packed = pl.pallas_call(
        backward_kernel,
        out_shape=shape(field, f32),
        in_specs=[SMEM, SMEM] + [VMEM] * 10,
        out_specs=VMEM,
        compiler_params=params(20),
        scratch_shapes=[
            pltpu.VMEM((32 * ROWS, 128), f32),
            pltpu.VMEM((32 * ROWS, 256), f32),
            pltpu.VMEM((32, ROWS, 128), f32),
        ],
        name="backward",
    )(gx, gy, mu, *tables, backward_weights(common), backward_weights(first), line, south, north, local)
    packed = lax.all_to_all(packed, "gx", split_axis=0, concat_axis=0, tiled=True)

    out = shape((8, LX, 128), f32)
    return pl.pallas_call(
        gradient_kernel,
        out_shape=(out, out, out),
        grid=(4,),
        in_specs=[SMEM, SMEM, whole((64, 128)), whole((104, 128)), whole(field), block, block, block],
        out_specs=(block, block, block),
        scratch_shapes=[pltpu.VMEM((8, 136, 128), f32), pltpu.VMEM((128, 128), f32)],
        compiler_params=params(16),
        name="gradient",
    )(gx, thickness, unmix, line, packed, u_vel, v_vel, w_vel)


def solution(mesh):
    return jax.shard_map(
        on_device,
        mesh=mesh,
        in_specs=(P(None, "gx", "gy"), P(None, "gx", "gy"), P(None, "gx", "gy"), P()),
        out_specs=(P(None, "gx", "gy"), P(None, "gx", "gy"), P(None, "gx", "gy")),
        check_vma=False,
    )
```

```python
import math

import jax
import jax.numpy as jnp
import numpy as np
from jax import lax
from jax.experimental import pallas as pl
from jax.experimental.pallas import tpu as pltpu
from jax.sharding import PartitionSpec as P

highest = lax.Precision.HIGHEST
f32 = jnp.float32
NX = 4096
NY = 4096
NZ = 8
LX = 512
ROWS = 136
BATCH = 4
PAY = 520
HALF = float(np.sqrt(0.5))

CLASSES = [0] + [mu + 16 * tau for mu in range(1, 8) for tau in range(4)] + [16, 8, 24]


def class_modes():
    t = np.arange(64)
    rows = [np.concatenate([64 * t, 64 * t + 32])]
    for nu in CLASSES[1:]:
        rows.append(np.concatenate([64 * t + nu, 64 * (t + 1) - nu]))
    return np.stack(rows)


def dct_tables():
    b = np.arange(128)[:, None]
    t = np.arange(64)[None, :]
    near = math.pi * t * (2 * b + 1) / 128
    far = math.pi * (t + 1) * (2 * b + 1) / 128
    common = np.block([[np.cos(near), np.cos(far)], [np.sin(near), -np.sin(far)]])
    zero = np.zeros((128, 64))
    middle = np.cos(math.pi * (64 * t + 32) * (2 * b + 1) / 8192)
    first = np.block([[np.cos(near), zero], [zero, middle]])
    nu = np.array(CLASSES)[:, None]
    angle = math.pi * nu * (2 * np.arange(128)[None, :] + 1) / 8192
    return common, first, np.cos(angle), np.sin(angle)


def line_tables():
    d = np.arange(32)
    j = np.arange(128)
    a32 = 2 * math.pi * (d[:, None] * d[None, :] % 32) / 32
    a128 = 2 * math.pi * (j[:, None] * j[None, :] % 128) / 128
    tw = 2 * math.pi * (d[:, None] * j[None, :]) / 4096
    q = d[:, None] + 32 * j[None, :]
    lam = -4.0 * np.sin(math.pi * q / NY) ** 2
    return np.cos(a32), np.sin(a32), np.cos(tw), np.sin(tw), np.cos(a128), np.sin(a128), lam


def three_parts(values):
    rest = np.asarray(values, dtype=np.float32)
    parts = []
    for _ in range(3):
        part = rest.astype(jnp.bfloat16)
        parts.append(part)
        rest = rest - part.astype(np.float32)
    return parts


def forward_weights(matrix):
    high, mid, low = three_parts(matrix)
    return jnp.asarray(np.concatenate([high, mid, low, np.zeros_like(low)], axis=1))


def backward_weights(matrix):
    high, mid, low = three_parts(matrix.T)
    return jnp.asarray(np.concatenate([high, high, mid, mid, low, high], axis=0))


def head(x):
    scaled = x * 65537.0
    return scaled - (scaled - x)


def split(x):
    high = x.astype(jnp.bfloat16)
    rest = x - high.astype(f32)
    mid = head(rest)
    return high, mid.astype(jnp.bfloat16), (rest - mid).astype(jnp.bfloat16)


def times_bf16(a, b):
    return jnp.dot(a, b, preferred_element_type=f32)


def forward_product(x, w_ref):
    high, mid, low = split(x)
    both = times_bf16(high, w_ref[:, 0:256]) + times_bf16(mid, w_ref[:, 0:256])
    rest = times_bf16(high, w_ref[:, 256:384]) + times_bf16(low, w_ref[:, 0:128])
    return both[:, 0:128] + (both[:, 128:256] + rest)


def backward_product(x, w_ref):
    high, mid, low = split(x)
    two = jnp.concatenate([high, mid], axis=1)
    rest = times_bf16(two, w_ref[256:512, :]) + times_bf16(jnp.concatenate([high, low], axis=1), w_ref[512:768, :])
    return times_bf16(two, w_ref[0:256, :]) + rest


def slow_table():
    slow = class_modes()[:, [0, 1, 2, 3, 64, 65, 66, 67]].T
    return np.sin(math.pi * np.tile(slow, (1, 4)) / 8192) ** 2


def const(values):
    return jnp.asarray(np.asarray(values, dtype=np.float32))


def across_blocks(x):
    e = [x[s] + x[s + 4] for s in range(4)]
    o = [x[s] - x[s + 4] for s in range(4)]
    out = [None] * 9
    e02, e13 = e[0] + e[2], e[1] + e[3]
    out[0] = e02 + e13
    out[8] = e02 - e13
    out[4] = (e[0] - e[2], e[3] - e[1])
    d13, s13 = HALF * (o[1] - o[3]), HALF * (o[1] + o[3])
    out[2] = (o[0] + d13, -o[2] - s13)
    out[6] = (o[0] - d13, o[2] - s13)
    zr, zi = [x[0]], [-x[4]]
    for s in (1, 2, 3):
        c, q = math.cos(math.pi * s / 8), math.sin(math.pi * s / 8)
        zr.append(x[s] * c - x[s + 4] * q)
        zi.append(-(x[s] * q + x[s + 4] * c))
    y = four(zr, zi)
    out[1] = y[0]
    out[5] = y[1]
    out[7] = (y[2][0], -y[2][1])
    out[3] = (y[3][0], -y[3][1])
    return out


def four(zr, zi):
    t0r, t0i = zr[0] + zr[2], zi[0] + zi[2]
    t1r, t1i = zr[0] - zr[2], zi[0] - zi[2]
    t2r, t2i = zr[1] + zr[3], zi[1] + zi[3]
    t3r, t3i = zr[1] - zr[3], zi[1] - zi[3]
    return [
        (t0r + t2r, t0i + t2i),
        (t1r + t3i, t1i - t3r),
        (t0r - t2r, t0i - t2i),
        (t1r - t3i, t1i + t3r),
    ]


def four_back(h):
    zr = [v[0] for v in h]
    zi = [v[1] for v in h]
    t0r, t0i = zr[0] + zr[2], zi[0] + zi[2]
    t1r, t1i = zr[0] - zr[2], zi[0] - zi[2]
    t2r, t2i = zr[1] + zr[3], zi[1] + zi[3]
    t3r, t3i = zr[1] - zr[3], zi[1] - zi[3]
    return [
        (t0r + t2r, t0i + t2i),
        (t1r - t3i, t1i + t3r),
        (t0r - t2r, t0i - t2i),
        (t1r + t3i, t1i - t3r),
    ]


def forward_classes(x):
    per_a = [across_blocks([x[4 * s + a] for s in range(8)]) for a in range(4)]
    out = []
    y0 = [per_a[a][0] for a in range(4)]
    y8 = [per_a[a][8] for a in range(4)]
    out.append(((y0[0] + y0[2]) + (y0[1] + y0[3]), (y0[0] + y0[2]) - (y0[1] + y0[3])))
    for mu in range(1, 8):
        zr, zi = [per_a[0][mu][0]], [per_a[0][mu][1]]
        for a in (1, 2, 3):
            yr, yi = per_a[a][mu]
            c, q = math.cos(math.pi * mu * a / 32), math.sin(math.pi * mu * a / 32)
            zr.append(yr * c + yi * q)
            zi.append(yi * c - yr * q)
        out.extend(four(zr, zi))
    out.append((y0[0] - y0[2], y0[3] - y0[1]))
    d13, s13 = HALF * (y8[1] - y8[3]), HALF * (y8[1] + y8[3])
    out.append((y8[0] + d13, -y8[2] - s13))
    out.append((y8[0] - d13, y8[2] - s13))
    return out


def backward_classes(h):
    h0, h32 = h[0]
    h16, h8, h24 = h[29], h[30], h[31]
    x = [None] * 32
    by_mu = {}
    for mu in range(1, 8):
        z = four_back(h[1 + 4 * (mu - 1) : 5 + 4 * (mu - 1)])
        for a in (1, 2, 3):
            c, q = math.cos(math.pi * mu * a / 32), math.sin(math.pi * mu * a / 32)
            zr, zi = z[a]
            z[a] = (zr * c - zi * q, zr * q + zi * c)
        by_mu[mu] = z
    sum0, dif0 = h0 + h32, h0 - h32
    y0 = [sum0 + h16[0], dif0 - h16[1], sum0 - h16[0], dif0 + h16[1]]
    dr, di = HALF * (h8[0] - h24[0]), HALF * (h8[1] + h24[1])
    y8 = [h8[0] + h24[0], dr - di, h24[1] - h8[1], -dr - di]
    for a in range(4):
        y = {mu: by_mu[mu][a] for mu in by_mu}
        ea, eb = y0[a] + y8[a], y0[a] - y8[a]
        y2, y4, y6 = y[2], y[4], y[6]
        rep = [ea + y4[0], eb - y4[1], ea - y4[0], eb + y4[1]]
        er, ei = HALF * (y2[0] - y6[0]), HALF * (y2[1] + y6[1])
        alt = [y2[0] + y6[0], er - ei, y6[1] - y2[1], -er - ei]
        u = four_back([y[1], y[5], (y[7][0], -y[7][1]), (y[3][0], -y[3][1])])
        for s in range(4):
            ur, ui = u[s]
            if s:
                c, q = math.cos(math.pi * s / 8), math.sin(math.pi * s / 8)
                ur, ui = ur * c - ui * q, ur * q + ui * c
            x[4 * s + a] = rep[s] + alt[s] + ur
            x[4 * (s + 4) + a] = rep[s] - alt[s] - ui
    return x


def decay(eigen):
    half = 0.5 * jnp.sqrt(-eigen)
    root = jnp.sqrt(1.0 + half * half)
    gap = 2.0 * half * (root - half)
    return 1.0 - gap, gap, -0.25 / (half * root)


def doubled(gap, times):
    for _ in range(times):
        gap = gap * (2.0 - gap)
    return gap


ROUNDS = []
_seats = list(range(8))
for _ in range(7):
    ROUNDS.append([tuple(sorted((_seats[i], _seats[7 - i]))) for i in range(4)])
    _seats = [_seats[0], _seats[7]] + _seats[1:7]
SWEEPS = 5
PAIRS = [(i, j) for i in range(8) for j in range(i, 8)]


def vertical_modes(thick_ref, mix_ref, unmix_ref, mu_ref):
    t = [jnp.full((8, 128), thick_ref[k], f32) for k in range(8)]
    unit = 16384.0
    zero = jnp.zeros((8, 128), f32)
    one = jnp.ones((8, 128), f32)
    centre = [0.5 * (t[k] + t[k + 1]) for k in range(7)]
    root = [jnp.sqrt(t[k]) for k in range(8)]
    a = {pair: zero for pair in PAIRS}
    for k in range(8):
        total = zero
        if k < 7:
            total = total + unit / (t[k] * centre[k])
            a[(k, k + 1)] = unit / (centre[k] * (root[k] * root[k + 1]))
        if k > 0:
            total = total + unit / (t[k] * centre[k - 1])
        a[(k, k)] = -total
    vec = [[one if i == j else zero for j in range(8)] for i in range(8)]

    def sweep(_, carry):
        flat_a, flat_v = carry
        a = dict(zip(PAIRS, flat_a))
        vec = [list(flat_v[8 * i : 8 * i + 8]) for i in range(8)]

        def get(i, j):
            return a[(i, j) if i <= j else (j, i)]

        for pairs in ROUNDS:
            turn = {}
            for p, q in pairs:
                off = a[(p, q)]
                diff = a[(q, q)] - a[(p, p)]
                twice = 2.0 * off
                square = diff * diff + twice * twice
                some = square > 0.0
                inv = lax.rsqrt(jnp.where(some, square, 1.0))
                both = 0.5 + 0.5 * jnp.where(some, jnp.abs(diff) * inv, 1.0)
                over = lax.rsqrt(both)
                cos = both * over
                sin = 0.5 * jnp.where(diff < 0.0, -twice, twice) * (inv * over)
                tan = sin * over
                turn[(p, q)] = (cos, sin, tan)
            new = {}
            for n, (p, q) in enumerate(pairs):
                cos, sin, tan = turn[(p, q)]
                off = a[(p, q)]
                new[(p, p)] = a[(p, p)] - tan * off
                new[(q, q)] = a[(q, q)] + tan * off
                new[(p, q)] = zero
                for i in range(8):
                    x, y = vec[i][p], vec[i][q]
                    vec[i][p], vec[i][q] = cos * x - sin * y, sin * x + cos * y
                for r, s in pairs[n + 1 :]:
                    cos2, sin2, _t = turn[(r, s)]
                    half = []
                    for i in (p, q):
                        x, y = get(i, r), get(i, s)
                        half.append((cos2 * x - sin2 * y, sin2 * x + cos2 * y))
                    for j, x, y in ((r, half[0][0], half[1][0]), (s, half[0][1], half[1][1])):
                        new[tuple(sorted((p, j)))] = cos * x - sin * y
                        new[tuple(sorted((q, j)))] = sin * x + cos * y
            a = new
        return tuple(a[pair] for pair in PAIRS), tuple(vec[i][j] for i in range(8) for j in range(8))

    start = (tuple(a[pair] for pair in PAIRS), tuple(vec[i][j] for i in range(8) for j in range(8)))
    flat_a, flat_v = lax.fori_loop(0, SWEEPS, sweep, start)
    a = dict(zip(PAIRS, flat_a))
    for mode in range(8):
        mu_ref[mode : mode + 1, :] = jnp.minimum(a[(mode, mode)] * (1.0 / unit), 0.0)[0:1]
        for k in range(8):
            entry = flat_v[8 * k + mode]
            mix_ref[8 * mode + k : 8 * mode + k + 1, :] = (entry * root[k])[0:1]
            unmix_ref[8 * k + mode : 8 * k + mode + 1, :] = (entry / root[k])[0:1]


def iota(shape, axis):
    return lax.broadcasted_iota(jnp.int32, shape, axis)


def divergence_kernel(
    gx_ref, thick_ref, u_hbm, v_hbm, w_hbm, out_ref, unmix_ref, mu_ref,
    mix_ref, u_ref, v_ref, w_ref, last_ref, sum_ref, sems,
):
    def copies(step):
        rows = pl.ds(128 * step, 128)
        return [
            pltpu.make_async_copy(src.at[:, rows, :], dst.at[:, rows, :], sems.at[n, step])
            for n, (src, dst) in enumerate(((u_hbm, u_ref), (v_hbm, v_ref), (w_hbm, w_ref)))
        ]

    for step in range(4):
        for copy in copies(step):
            copy.start()
    vertical_modes(thick_ref, mix_ref, unmix_ref, mu_ref)

    last_ref[...] = jnp.zeros((64, 128), f32)
    sum_ref[...] = jnp.zeros((64, 128), f32)
    lane = iota((16, 128), 1)
    row = iota((16, 128), 0)
    lanes = iota((128, 128), 1)
    ones = jnp.ones((1, 128), f32)
    inverse = [1.0 / (ones * thick_ref[k]) for k in range(8)]

    def block(step, carry):
        for copy in copies(step):
            copy.wait()
        wall = jnp.logical_and(gx_ref[0] == 7, step == 3)
        base = pl.multiple_of(step * 128, 128)
        for sub in range(8):
            rows = pl.ds(base + 16 * sub, 16)
            div = []
            below = None
            for k in range(8):
                u = u_ref[k, rows, :]
                if sub == 7:
                    u = jnp.where(jnp.logical_and(wall, row == 15), 0.0, u)
                prev = pltpu.roll(u, 1, axis=0)
                prev = jnp.where(row == 0, last_ref[8 * k : 8 * k + 1, :], prev)
                last_ref[8 * k : 8 * k + 1, :] = u[15:16]
                v = v_ref[k, rows, :]
                back = jnp.where(lane == 0, 0.0, pltpu.roll(v, 1, axis=1))
                if k < 7:
                    w = w_ref[k, rows, :]
                    up = w if below is None else w - below
                    below = w
                else:
                    up = -below
                rise = up * inverse[k]
                sum_ref[8 * k : 8 * k + 8, :] += rise[0:8] + rise[8:16]
                div.append((u - prev) + (v - back) + rise)
            for mode in range(8):
                acc = div[0] * mix_ref[8 * mode : 8 * mode + 1, :]
                for k in range(1, 8):
                    acc = acc + div[k] * mix_ref[8 * mode + k : 8 * mode + k + 1, :]
                out_ref[mode, rows, :] = acc

        edge = jnp.zeros((128, 128), f32)
        for k in range(8):
            edge = jnp.where(lanes == k, pltpu.roll(v_ref[k, pl.ds(base, 128), :], k + 1, axis=1), edge)
        edge = edge.T
        for mode in range(8):
            acc = edge[0:1] * mix_ref[8 * mode : 8 * mode + 1, :]
            for k in range(1, 8):
                acc = acc + edge[k : k + 1] * mix_ref[8 * mode + k : 8 * mode + k + 1, :]
            out_ref[mode, pl.ds(513 + step, 1), :] = -acc
        return carry

    lax.fori_loop(0, 4, block, 0)

    lane1 = iota((1, 128), 1)
    totals = jnp.zeros((1, 128), f32)
    for k in range(8):
        part = jnp.sum(sum_ref[8 * k : 8 * k + 8, :], axis=0, keepdims=True)
        part = jnp.sum(part, axis=1, keepdims=True)
        totals = jnp.where(lane1 == k, part, totals)
    for mode in range(8):
        acc = last_ref[0:1, :] * mix_ref[8 * mode : 8 * mode + 1, :]
        for k in range(1, 8):
            acc = acc + last_ref[8 * k : 8 * k + 1, :] * mix_ref[8 * mode + k : 8 * mode + k + 1, :]
        out_ref[mode, 512:513, :] = acc
        out_ref[mode, 517:518, :] = totals
        out_ref[mode, 518:520, :] = jnp.zeros((2, 128), f32)


def eigen_table(sines, mu_row, with_first):
    eigen = mu_row - 4.0 * sines
    if with_first:
        first = jnp.logical_and(iota(sines.shape, 0) == 0, iota(sines.shape, 1) == 0)
        eigen = jnp.where(first, -1.0, eigen)
    return eigen


def forward_kernel(
    gx_ref, mu_ref, sines_ref, tc_ref, ts_ref, common_ref, first_ref, in_ref, out_ref, small_ref,
    south_ref, north_ref, grid_ref, y_ref, raw_ref, side_ref, turn_ref,
):
    row8 = iota((8, 128), 0)
    row128 = iota((128, 128), 0)
    for s in range(8):
        for part in range(4):
            tile = in_ref[s, 128 * part : 128 * part + 128, :]
            if part == 0 and s > 0:
                tile = jnp.where(row128 == 0, tile - in_ref[s - 1, 512:513, :], tile)
            grid_ref[4 * s + part, 0:128, :] = tile.T
            ghost = in_ref[s, 513 + part : 514 + part, :]
            grid_ref[4 * s + part, 128:136, :] = jnp.where(row8 == 0, ghost, 0.0)

    def group(i, carry):
        start = pl.multiple_of(i * 8, 8)
        y = forward_classes([grid_ref[g, pl.ds(start, 8), :] for g in range(32)])
        y_ref[pl.ds(start, 8), 0:128] = y[0][0]
        y_ref[pl.ds(start, 8), 128:256] = y[0][1]
        for c in range(1, 32):
            re, im = y[c]
            tc, ts = tc_ref[c : c + 1, :], ts_ref[c : c + 1, :]
            rows = pl.ds(start + ROWS * c, 8)
            y_ref[rows, 0:128] = re * tc + im * ts
            y_ref[rows, 128:256] = im * tc - re * ts
        return carry

    lax.fori_loop(0, ROWS // 8, group, 0)

    batch = BATCH * ROWS

    def product(n, carry):
        start = pl.multiple_of(n * batch, 8)
        raw_ref[pl.ds(start, batch), :] = forward_product(y_ref[pl.ds(start, batch), :], common_ref)
        return carry

    lax.fori_loop(0, 32 // BATCH, product, 0)
    raw_ref[0:144, :] = jnp.where(
        iota((144, 128), 0) < ROWS, forward_product(y_ref[0:144, :], first_ref), raw_ref[0:144, :]
    )

    line = raw_ref[0:128, :].T[0:1]
    ghost_line = raw_ref[128:129, :]

    eigen = eigen_table(sines_ref[...], mu_ref[pl.ds(gx_ref[0], 1), :], True)
    rho, gap, _ = decay(eigen)
    ghost = raw_ref[pl.ds(128, 32, stride=ROWS), :]

    def from_north(n, b):
        j = 127 - n
        side_ref[pl.ds(j, 32, stride=ROWS), :] = rho * b
        return raw_ref[pl.ds(j, 32, stride=ROWS), :] + (b - gap * b)

    b = lax.fori_loop(0, 128, from_north, ghost, unroll=8)

    def from_south(j, f):
        f = raw_ref[pl.ds(j, 32, stride=ROWS), :] + (f - gap * f)
        out_ref[pl.ds(j, 32, stride=ROWS), :] = f + side_ref[pl.ds(j, 32, stride=ROWS), :]
        return f

    f = lax.fori_loop(0, 128, from_south, jnp.zeros((32, 128), f32), unroll=8)
    out_ref[pl.ds(128, 32, stride=ROWS), :] = rho * f + ghost
    for r in range(129, ROWS):
        out_ref[pl.ds(r, 32, stride=ROWS), :] = jnp.zeros((32, 128), f32)

    totals = in_ref[0, 517:518, :]
    for s in range(1, 8):
        totals = totals + in_ref[s, 517:518, :]
    f = f + ghost / rho
    south_ref[...] = f
    north_ref[...] = b
    turn_ref[0:32, :] = f
    turn_ref[32:64, :] = b
    turn_ref[64:128, :] = jnp.zeros((64, 128), f32)
    turn_ref[...] = turn_ref[...].T
    turn_ref[4:8, :] = turn_ref[64:68, :]
    lane1 = iota((1, 128), 1)
    extra = [pltpu.roll(line, 64, axis=1), line, pltpu.roll(totals, 64, axis=1), pltpu.roll(ghost_line, 64, axis=1)]
    for r in range(4):
        turn_ref[r : r + 1, :] = jnp.where(lane1 < 64, turn_ref[r : r + 1, :], extra[r])
    for d in range(32):
        small_ref[8 * d : 8 * d + 8, :] = turn_ref[0:8, :]


def line_kernel(
    gx_ref, gy_ref, thick_ref, mu_ref, slow_ref, c32_ref, s32_ref, tc_ref, ts_ref, c128_ref, s128_ref, lam_ref,
    in_ref, out_ref, turn_ref,
):
    def times(a, b):
        return jnp.dot(a, b, precision=highest, preferred_element_type=f32)

    own = gy_ref[0]
    eigen = mu_ref[pl.ds(gx_ref[0], 1), :] - 4.0 * slow_ref[...]
    lane8 = iota((8, 128), 1)
    first = jnp.logical_and(iota((8, 128), 0) == 0, lane8 % 32 == 0)
    _, gap, _ = decay(jnp.where(first, -1.0, eigen))
    gap_block = doubled(gap, 7)
    around = 1.0 / doubled(gap_block, 5)
    c = jnp.zeros((8, 128), f32)
    h = jnp.zeros((8, 128), f32)
    for e in range(32, 0, -1):
        c = in_ref[pl.ds(pl.multiple_of((own + 32 - e) % 32 * 8, 8), 8), :] + (c - gap_block * c)
        h = in_ref[pl.ds(pl.multiple_of((own + e) % 32 * 8, 8), 8), :] + (h - gap_block * h)
    carry = jnp.where(lane8 < 32, c, h) * around
    turn_ref[...] = jnp.zeros((128, 128), f32)
    turn_ref[0:4, :] = carry[0:4]
    turn_ref[64:68, :] = carry[4:8]
    out_ref[40:104, :] = turn_ref[...].T[0:64]

    lane32 = iota((32, 128), 1)
    line = jnp.where(
        lane32 < 64,
        pltpu.roll(in_ref[pl.ds(0, 32, stride=8), :], 64, axis=1),
        in_ref[pl.ds(1, 32, stride=8), :],
    )
    ghost = pltpu.roll(in_ref[pl.ds(3, 32, stride=8), :], 64, axis=1)
    at_first = iota((32, 128), 1) == 0
    line = line + jnp.where(at_first, pltpu.roll(ghost, 1, axis=0), 0.0)
    c32, s32 = c32_ref[...], s32_ref[...]
    tc, ts = tc_ref[...], ts_ref[...]
    c128, s128 = c128_ref[...], s128_ref[...]
    re, im = times(c32, line), -times(s32, line)
    re, im = re * tc + im * ts, im * tc - re * ts
    re, im = times(re, c128) + times(im, s128), times(im, c128) - times(re, s128)
    mean = jnp.logical_and(iota((32, 128), 0) == 0, at_first)
    eigen = mu_ref[pl.ds(gx_ref[0], 1), :] + lam_ref[...]
    gain = jnp.where(mean, 0.0, (1.0 / NY) / jnp.where(mean, 1.0, eigen))
    re, im = re * gain, im * gain
    re, im = times(re, c128) - times(im, s128), times(im, c128) + times(re, s128)
    re, im = re * tc - im * ts, im * tc + re * ts
    out_ref[0:32, :] = times(c32, re) - times(s32, im)

    totals = jnp.sum(in_ref[pl.ds(2, 32, stride=8), :], axis=0, keepdims=True)
    totals = pltpu.roll(totals, 64, axis=1)
    lane = iota((1, 128), 1)
    ones = jnp.ones((1, 128), f32)
    rhs = [ones * jnp.sum(jnp.where(lane == k, totals, 0.0), axis=1, keepdims=True) for k in range(8)]
    t = [ones * thick_ref[k] for k in range(8)]
    centre = [0.5 * (t[k] + t[k + 1]) for k in range(7)]
    zero = jnp.zeros((1, 128), f32)
    upper = [1.0 / (t[k] * centre[k]) for k in range(7)] + [zero]
    lower = [zero] + [1.0 / (t[k] * centre[k - 1]) for k in range(1, 8)]
    reduced, ratio = [], []
    excess = zero
    for k in range(8):
        if k == 0:
            excess = -upper[0]
            top = rhs[0]
        else:
            excess = lower[k] * excess / (upper[k - 1] - excess)
            top = rhs[k] - lower[k] * reduced[-1]
        pivot = excess - upper[k]
        reduced.append(top / pivot)
        ratio.append(upper[k] / pivot)
    value = zero
    for k in reversed(range(8)):
        value = reduced[k] - ratio[k] * value
        out_ref[32 + k : 33 + k, :] = value * (1.0 / NX) * (1.0 / NY)


def backward_kernel(
    gx_ref, gy_ref, mu_ref, sines_ref, tc_ref, ts_ref, common_ref, first_ref, line_ref, south_ref,
    north_ref, in_ref, out_ref, half_ref, p_ref, z_ref, grid_ref,
):
    eigen = eigen_table(sines_ref[...], mu_ref[pl.ds(gx_ref[0], 1), :], True)
    rho, gap, factor = decay(eigen)
    at_zero = jnp.logical_and(iota((32, 128), 0) == 0, iota((32, 128), 1) == 0)
    factor = factor * jnp.where(at_zero, 1.0 / NX, 2.0 / NX)
    slow = iota((32, 128), 1) % 64 < 4
    south = jnp.where(slow, line_ref[40:72, :], south_ref[...])
    north = jnp.where(slow, line_ref[72:104, :], north_ref[...])

    def from_south(j, c):
        c = c - gap * c
        half_ref[pl.ds(j, 32, stride=ROWS), :] = in_ref[pl.ds(j, 32, stride=ROWS), :] + c
        return c

    c = lax.fori_loop(0, 128, from_south, south, unroll=8)
    c = c - gap * c
    p_ref[pl.ds(128, 32, stride=ROWS), :] = (in_ref[pl.ds(128, 32, stride=ROWS), :] + c + north) * factor

    def from_north(n, h):
        j = 127 - n
        h = h - gap * h
        p_ref[pl.ds(j, 32, stride=ROWS), :] = (half_ref[pl.ds(j, 32, stride=ROWS), :] + h) * factor
        return h

    lax.fori_loop(0, 128, from_north, north, unroll=8)
    for r in range(129, ROWS):
        p_ref[pl.ds(r, 32, stride=ROWS), :] = jnp.zeros((32, 128), f32)

    own = gy_ref[0]
    line = line_ref[pl.ds(own, 1), :] * (1.0 / NX)
    after = line_ref[pl.ds((own + 1) % 32, 1), :] * (1.0 / NX)
    lane128 = iota((128, 128), 1)
    column = jnp.where(iota((128, 128), 0) == 0, line, 0.0).T
    p_ref[0:128, :] = jnp.where(lane128 == 0, column, p_ref[0:128, :])
    lane1 = iota((1, 128), 1)
    p_ref[128:129, :] = jnp.where(lane1 == 0, after, p_ref[128:129, :])

    batch = BATCH * ROWS

    def product(n, carry):
        start = pl.multiple_of(n * batch, 8)
        z_ref[pl.ds(start, batch), :] = backward_product(p_ref[pl.ds(start, batch), :], common_ref)
        return carry

    lax.fori_loop(0, 32 // BATCH, product, 0)
    z_ref[0:ROWS, :] = backward_product(p_ref[0:144, :], first_ref)[0:ROWS]

    def group(i, carry):
        start = pl.multiple_of(i * 8, 8)
        rows = pl.ds(start, 8)
        h = [(z_ref[rows, 0:128], z_ref[rows, 128:256])]
        for c in range(1, 32):
            part = pl.ds(start + ROWS * c, 8)
            re, im = z_ref[part, 0:128], z_ref[part, 128:256]
            tc, ts = tc_ref[c : c + 1, :], ts_ref[c : c + 1, :]
            h.append((re * tc - im * ts, im * tc + re * ts))
        x = backward_classes(h)
        for g in range(32):
            grid_ref[g, rows, :] = x[g]
        return carry

    lax.fori_loop(0, ROWS // 8, group, 0)

    for s in range(8):
        for part in range(4):
            tile = grid_ref[4 * s + part, 0:128, :].T
            out_ref[s, 128 * part : 128 * part + 128, :] = tile
            if part == 0 and s > 0:
                out_ref[s - 1, 512:513, :] = tile[0:1]
            out_ref[s, 513 + part : 514 + part, :] = grid_ref[4 * s + part, 128:129, :]
        out_ref[s, 517:520, :] = jnp.zeros((3, 128), f32)
    out_ref[7, 512:513, :] = jnp.zeros((1, 128), f32)


def gradient_kernel(
    gx_ref, thick_ref, unmix_ref, line_ref, p_ref, u_ref, v_ref, w_ref, uo_ref, vo_ref, wo_ref, press_ref, edge_ref
):
    step = pl.program_id(0)
    base = pl.multiple_of(step * 128, 128)
    wall = jnp.logical_and(gx_ref[0] == 7, step == 3)
    edge_ref[...] = jnp.zeros((128, 128), f32)
    for k in range(8):
        acc = p_ref[0, pl.ds(513 + step, 1), :] * unmix_ref[8 * k : 8 * k + 1, :]
        for mode in range(1, 8):
            acc = acc + p_ref[mode, pl.ds(513 + step, 1), :] * unmix_ref[8 * k + mode : 8 * k + mode + 1, :]
        edge_ref[k : k + 1, :] = acc
    edge_ref[...] = edge_ref[...].T
    for sub in range(17):
        parts = [p_ref[mode, pl.ds(base + 8 * sub, 8), :] for mode in range(8)]
        for k in range(8):
            acc = parts[0] * unmix_ref[8 * k : 8 * k + 1, :]
            for mode in range(1, 8):
                acc = acc + parts[mode] * unmix_ref[8 * k + mode : 8 * k + mode + 1, :]
            press_ref[k, 8 * sub : 8 * sub + 8, :] = acc
    lane = iota((16, 128), 1)
    row = iota((16, 128), 0)
    ones = jnp.ones((1, 128), f32)
    t = [ones * thick_ref[k] for k in range(8)]
    inverse = [2.0 / (t[k] + t[k + 1]) for k in range(7)]
    drift = [(line_ref[33 + k : 34 + k, :] - line_ref[32 + k : 33 + k, :]) * inverse[k] for k in range(7)]
    for sub in range(8):
        rows = slice(16 * sub, 16 * sub + 16)
        edge = edge_ref[rows, :]
        for k in range(8):
            p = press_ref[k, rows, :]
            east = press_ref[k, 16 * sub + 1 : 16 * sub + 17, :]
            u = u_ref[k, rows, :] - (east - p)
            if sub == 7:
                u = jnp.where(jnp.logical_and(wall, row == 15), 0.0, u)
            uo_ref[k, rows, :] = u
            north = jnp.where(lane == 127, pltpu.roll(edge, 127 - k, axis=1), pltpu.roll(p, 127, axis=1))
            vo_ref[k, rows, :] = v_ref[k, rows, :] - (north - p)
            if k < 7:
                wo_ref[k, rows, :] = w_ref[k, rows, :] - ((press_ref[k + 1, rows, :] - p) * inverse[k] + drift[k])
            else:
                wo_ref[k, rows, :] = jnp.zeros((16, 128), f32)


SMEM = pl.BlockSpec(memory_space=pltpu.SMEM)
VMEM = pl.BlockSpec(memory_space=pltpu.VMEM)


def params(mib):
    return pltpu.CompilerParams(vmem_limit_bytes=mib * 2**20)


def whole(shape):
    return pl.BlockSpec(shape, lambda i: (0,) * len(shape))


def on_device(u_vel, v_vel, w_vel, thickness):
    gx = lax.axis_index("gx").astype(jnp.int32)[None]
    gy = lax.axis_index("gy").astype(jnp.int32)[None]
    common, first, tc, ts = dct_tables()
    sines = const(np.sin(math.pi * class_modes() / 8192) ** 2)
    tables = (sines, const(tc), const(ts))
    shape = jax.ShapeDtypeStruct

    block = pl.BlockSpec((8, 128, 128), lambda i: (0, i, 0))
    field = (8, PAY, 128)
    local_field = pltpu.VMEM((8, LX, 128), f32)
    packed, unmix, mu = pl.pallas_call(
        divergence_kernel,
        out_shape=(shape(field, f32), shape((64, 128), f32), shape((8, 128), f32)),
        in_specs=[SMEM, SMEM] + [pl.BlockSpec(memory_space=pltpu.HBM)] * 3,
        out_specs=(VMEM, VMEM, VMEM),
        scratch_shapes=[
            pltpu.VMEM((64, 128), f32),
            local_field,
            local_field,
            local_field,
            pltpu.VMEM((64, 128), f32),
            pltpu.VMEM((64, 128), f32),
            pltpu.SemaphoreType.DMA((3, 4)),
        ],
        compiler_params=params(12),
        name="divergence",
    )(gx, thickness, *[pltpu.with_memory_space_constraint(x, pltpu.HBM) for x in (u_vel, v_vel, w_vel)])
    packed = lax.all_to_all(packed, "gx", split_axis=0, concat_axis=0, tiled=True)

    rows = shape((32, 128), f32)
    local, small, south, north = pl.pallas_call(
        forward_kernel,
        out_shape=(shape((32 * ROWS, 128), f32), shape((256, 128), f32), rows, rows),
        in_specs=[SMEM] + [VMEM] * 7,
        out_specs=(VMEM, VMEM, VMEM, VMEM),
        scratch_shapes=[
            pltpu.VMEM((32, ROWS, 128), f32),
            pltpu.VMEM((32 * ROWS, 256), f32),
            pltpu.VMEM((32 * ROWS, 128), f32),
            pltpu.VMEM((32 * ROWS, 128), f32),
            pltpu.VMEM((128, 128), f32),
        ],
        compiler_params=params(20),
        name="forward",
    )(gx, mu, *tables, forward_weights(common), forward_weights(first), packed)
    small = lax.all_to_all(small, "gy", split_axis=0, concat_axis=0, tiled=True)

    parts = lax.axis_size("gy")
    south = lax.ppermute(south, "gy", [(i, (i + 1) % parts) for i in range(parts)])
    north = lax.ppermute(north, "gy", [(i, (i - 1) % parts) for i in range(parts)])
    line = pl.pallas_call(
        line_kernel,
        out_shape=shape((104, 128), f32),
        in_specs=[SMEM, SMEM, SMEM] + [VMEM] * 10,
        out_specs=VMEM,
        scratch_shapes=[pltpu.VMEM((128, 128), f32)],
        compiler_params=params(4),
        name="line",
    )(gx, gy, thickness, mu, const(slow_table()), *[const(x) for x in line_tables()], small)

    packed = pl.pallas_call(
        backward_kernel,
        out_shape=shape(field, f32),
        in_specs=[SMEM, SMEM] + [VMEM] * 10,
        out_specs=VMEM,
        compiler_params=params(20),
        scratch_shapes=[
            pltpu.VMEM((32 * ROWS, 128), f32),
            pltpu.VMEM((32 * ROWS, 128), f32),
            pltpu.VMEM((32 * ROWS, 256), f32),
            pltpu.VMEM((32, ROWS, 128), f32),
        ],
        name="backward",
    )(gx, gy, mu, *tables, backward_weights(common), backward_weights(first), line, south, north, local)
    packed = lax.all_to_all(packed, "gx", split_axis=0, concat_axis=0, tiled=True)

    out = shape((8, LX, 128), f32)
    return pl.pallas_call(
        gradient_kernel,
        out_shape=(out, out, out),
        grid=(4,),
        in_specs=[SMEM, SMEM, whole((64, 128)), whole((104, 128)), whole(field), block, block, block],
        out_specs=(block, block, block),
        scratch_shapes=[pltpu.VMEM((8, 136, 128), f32), pltpu.VMEM((128, 128), f32)],
        compiler_params=params(16),
        name="gradient",
    )(gx, thickness, unmix, line, packed, u_vel, v_vel, w_vel)


def solution(mesh):
    return jax.shard_map(
        on_device,
        mesh=mesh,
        in_specs=(P(None, "gx", "gy"), P(None, "gx", "gy"), P(None, "gx", "gy"), P()),
        out_specs=(P(None, "gx", "gy"), P(None, "gx", "gy"), P(None, "gx", "gy")),
        check_vma=False,
    )
```

```python
import math

import jax
import jax.numpy as jnp
import numpy as np
from jax import lax
from jax.experimental import pallas as pl
from jax.experimental.pallas import tpu as pltpu
from jax.sharding import PartitionSpec as P

highest = lax.Precision.HIGHEST
f32 = jnp.float32
NX = 4096
NY = 4096
NZ = 8
LX = 512
ROWS = 136
BATCH = 4
PAY = 520
HALF = float(np.sqrt(0.5))

CLASSES = [0] + [mu + 16 * tau for mu in range(1, 8) for tau in range(4)] + [16, 8, 24]


def class_modes():
    t = np.arange(64)
    rows = [np.concatenate([64 * t, 64 * t + 32])]
    for nu in CLASSES[1:]:
        rows.append(np.concatenate([64 * t + nu, 64 * (t + 1) - nu]))
    return np.stack(rows)


def dct_tables():
    b = np.arange(128)[:, None]
    t = np.arange(64)[None, :]
    near = math.pi * t * (2 * b + 1) / 128
    far = math.pi * (t + 1) * (2 * b + 1) / 128
    common = np.block([[np.cos(near), np.cos(far)], [np.sin(near), -np.sin(far)]])
    zero = np.zeros((128, 64))
    middle = np.cos(math.pi * (64 * t + 32) * (2 * b + 1) / 8192)
    first = np.block([[np.cos(near), zero], [zero, middle]])
    nu = np.array(CLASSES)[:, None]
    angle = math.pi * nu * (2 * np.arange(128)[None, :] + 1) / 8192
    return common, first, np.cos(angle), np.sin(angle)


def line_tables():
    d = np.arange(32)
    j = np.arange(128)
    a32 = 2 * math.pi * (d[:, None] * d[None, :] % 32) / 32
    a128 = 2 * math.pi * (j[:, None] * j[None, :] % 128) / 128
    tw = 2 * math.pi * (d[:, None] * j[None, :]) / 4096
    q = d[:, None] + 32 * j[None, :]
    lam = -4.0 * np.sin(math.pi * q / NY) ** 2
    return np.cos(a32), np.sin(a32), np.cos(tw), np.sin(tw), np.cos(a128), np.sin(a128), lam


def three_parts(values):
    rest = np.asarray(values, dtype=np.float32)
    parts = []
    for _ in range(3):
        part = rest.astype(jnp.bfloat16)
        parts.append(part)
        rest = rest - part.astype(np.float32)
    return parts


def forward_weights(matrix):
    high, mid, low = three_parts(matrix)
    return jnp.asarray(np.concatenate([high, mid, low, np.zeros_like(low)], axis=1))


def backward_weights(matrix):
    high, mid, low = three_parts(matrix.T)
    return jnp.asarray(np.concatenate([high, high, mid, mid, low, high], axis=0))


def head(x):
    scaled = x * 65537.0
    return scaled - (scaled - x)


def split(x):
    high = x.astype(jnp.bfloat16)
    rest = x - high.astype(f32)
    mid = head(rest)
    return high, mid.astype(jnp.bfloat16), (rest - mid).astype(jnp.bfloat16)


def times_bf16(a, b):
    return jnp.dot(a, b, preferred_element_type=f32)


def forward_product(x, w_ref):
    high, mid, low = split(x)
    both = times_bf16(high, w_ref[:, 0:256]) + times_bf16(mid, w_ref[:, 0:256])
    rest = times_bf16(high, w_ref[:, 256:384]) + times_bf16(low, w_ref[:, 0:128])
    return both[:, 0:128] + (both[:, 128:256] + rest)


def backward_product(x, w_ref):
    high, mid, low = split(x)
    two = jnp.concatenate([high, mid], axis=1)
    rest = times_bf16(two, w_ref[256:512, :]) + times_bf16(jnp.concatenate([high, low], axis=1), w_ref[512:768, :])
    return times_bf16(two, w_ref[0:256, :]) + rest


def slow_table():
    slow = class_modes()[:, [0, 1, 2, 3, 64, 65, 66, 67]].T
    return np.sin(math.pi * np.tile(slow, (1, 4)) / 8192) ** 2


def const(values):
    return jnp.asarray(np.asarray(values, dtype=np.float32))


def across_blocks(x):
    e = [x[s] + x[s + 4] for s in range(4)]
    o = [x[s] - x[s + 4] for s in range(4)]
    out = [None] * 9
    e02, e13 = e[0] + e[2], e[1] + e[3]
    out[0] = e02 + e13
    out[8] = e02 - e13
    out[4] = (e[0] - e[2], e[3] - e[1])
    d13, s13 = HALF * (o[1] - o[3]), HALF * (o[1] + o[3])
    out[2] = (o[0] + d13, -o[2] - s13)
    out[6] = (o[0] - d13, o[2] - s13)
    zr, zi = [x[0]], [-x[4]]
    for s in (1, 2, 3):
        c, q = math.cos(math.pi * s / 8), math.sin(math.pi * s / 8)
        zr.append(x[s] * c - x[s + 4] * q)
        zi.append(-(x[s] * q + x[s + 4] * c))
    y = four(zr, zi)
    out[1] = y[0]
    out[5] = y[1]
    out[7] = (y[2][0], -y[2][1])
    out[3] = (y[3][0], -y[3][1])
    return out


def four(zr, zi):
    t0r, t0i = zr[0] + zr[2], zi[0] + zi[2]
    t1r, t1i = zr[0] - zr[2], zi[0] - zi[2]
    t2r, t2i = zr[1] + zr[3], zi[1] + zi[3]
    t3r, t3i = zr[1] - zr[3], zi[1] - zi[3]
    return [
        (t0r + t2r, t0i + t2i),
        (t1r + t3i, t1i - t3r),
        (t0r - t2r, t0i - t2i),
        (t1r - t3i, t1i + t3r),
    ]


def four_back(h):
    zr = [v[0] for v in h]
    zi = [v[1] for v in h]
    t0r, t0i = zr[0] + zr[2], zi[0] + zi[2]
    t1r, t1i = zr[0] - zr[2], zi[0] - zi[2]
    t2r, t2i = zr[1] + zr[3], zi[1] + zi[3]
    t3r, t3i = zr[1] - zr[3], zi[1] - zi[3]
    return [
        (t0r + t2r, t0i + t2i),
        (t1r - t3i, t1i + t3r),
        (t0r - t2r, t0i - t2i),
        (t1r + t3i, t1i - t3r),
    ]


def forward_classes(x):
    per_a = [across_blocks([x[4 * s + a] for s in range(8)]) for a in range(4)]
    out = []
    y0 = [per_a[a][0] for a in range(4)]
    y8 = [per_a[a][8] for a in range(4)]
    out.append(((y0[0] + y0[2]) + (y0[1] + y0[3]), (y0[0] + y0[2]) - (y0[1] + y0[3])))
    for mu in range(1, 8):
        zr, zi = [per_a[0][mu][0]], [per_a[0][mu][1]]
        for a in (1, 2, 3):
            yr, yi = per_a[a][mu]
            c, q = math.cos(math.pi * mu * a / 32), math.sin(math.pi * mu * a / 32)
            zr.append(yr * c + yi * q)
            zi.append(yi * c - yr * q)
        out.extend(four(zr, zi))
    out.append((y0[0] - y0[2], y0[3] - y0[1]))
    d13, s13 = HALF * (y8[1] - y8[3]), HALF * (y8[1] + y8[3])
    out.append((y8[0] + d13, -y8[2] - s13))
    out.append((y8[0] - d13, y8[2] - s13))
    return out


def backward_classes(h):
    h0, h32 = h[0]
    h16, h8, h24 = h[29], h[30], h[31]
    x = [None] * 32
    by_mu = {}
    for mu in range(1, 8):
        z = four_back(h[1 + 4 * (mu - 1) : 5 + 4 * (mu - 1)])
        for a in (1, 2, 3):
            c, q = math.cos(math.pi * mu * a / 32), math.sin(math.pi * mu * a / 32)
            zr, zi = z[a]
            z[a] = (zr * c - zi * q, zr * q + zi * c)
        by_mu[mu] = z
    sum0, dif0 = h0 + h32, h0 - h32
    y0 = [sum0 + h16[0], dif0 - h16[1], sum0 - h16[0], dif0 + h16[1]]
    dr, di = HALF * (h8[0] - h24[0]), HALF * (h8[1] + h24[1])
    y8 = [h8[0] + h24[0], dr - di, h24[1] - h8[1], -dr - di]
    for a in range(4):
        y = {mu: by_mu[mu][a] for mu in by_mu}
        ea, eb = y0[a] + y8[a], y0[a] - y8[a]
        y2, y4, y6 = y[2], y[4], y[6]
        rep = [ea + y4[0], eb - y4[1], ea - y4[0], eb + y4[1]]
        er, ei = HALF * (y2[0] - y6[0]), HALF * (y2[1] + y6[1])
        alt = [y2[0] + y6[0], er - ei, y6[1] - y2[1], -er - ei]
        u = four_back([y[1], y[5], (y[7][0], -y[7][1]), (y[3][0], -y[3][1])])
        for s in range(4):
            ur, ui = u[s]
            if s:
                c, q = math.cos(math.pi * s / 8), math.sin(math.pi * s / 8)
                ur, ui = ur * c - ui * q, ur * q + ui * c
            x[4 * s + a] = rep[s] + alt[s] + ur
            x[4 * (s + 4) + a] = rep[s] - alt[s] - ui
    return x


def decay(eigen):
    half = 0.5 * jnp.sqrt(-eigen)
    root = jnp.sqrt(1.0 + half * half)
    gap = 2.0 * half * (root - half)
    return 1.0 - gap, gap, -0.25 / (half * root)


def doubled(gap, times):
    for _ in range(times):
        gap = gap * (2.0 - gap)
    return gap


ROUNDS = []
_seats = list(range(8))
for _ in range(7):
    ROUNDS.append([tuple(sorted((_seats[i], _seats[7 - i]))) for i in range(4)])
    _seats = [_seats[0], _seats[7]] + _seats[1:7]
SWEEPS = 5
PAIRS = [(i, j) for i in range(8) for j in range(i, 8)]


def vertical_modes(thick_ref, mix_ref, unmix_ref, mu_ref):
    t = [jnp.full((8, 128), thick_ref[k], f32) for k in range(8)]
    unit = 16384.0
    zero = jnp.zeros((8, 128), f32)
    one = jnp.ones((8, 128), f32)
    centre = [0.5 * (t[k] + t[k + 1]) for k in range(7)]
    root = [jnp.sqrt(t[k]) for k in range(8)]
    a = {pair: zero for pair in PAIRS}
    for k in range(8):
        total = zero
        if k < 7:
            total = total + unit / (t[k] * centre[k])
            a[(k, k + 1)] = unit / (centre[k] * (root[k] * root[k + 1]))
        if k > 0:
            total = total + unit / (t[k] * centre[k - 1])
        a[(k, k)] = -total
    place = iota((8, 128), 0)
    vec = [jnp.where(place == j, one, zero) for j in range(8)]
    scale = root[0]
    for k in range(1, 8):
        scale = jnp.where(place == k, root[k], scale)

    def sweep(_, carry):
        flat_a, flat_v = carry
        a = dict(zip(PAIRS, flat_a))
        vec = list(flat_v)

        def get(i, j):
            return a[(i, j) if i <= j else (j, i)]

        for pairs in ROUNDS:
            turn = {}
            for p, q in pairs:
                off = a[(p, q)]
                diff = a[(q, q)] - a[(p, p)]
                twice = 2.0 * off
                square = diff * diff + twice * twice
                some = square > 0.0
                inv = lax.rsqrt(jnp.where(some, square, 1.0))
                both = 0.5 + 0.5 * jnp.where(some, jnp.abs(diff) * inv, 1.0)
                over = lax.rsqrt(both)
                cos = both * over
                sin = 0.5 * jnp.where(diff < 0.0, -twice, twice) * (inv * over)
                tan = sin * over
                turn[(p, q)] = (cos, sin, tan)
            new = {}
            for n, (p, q) in enumerate(pairs):
                cos, sin, tan = turn[(p, q)]
                off = a[(p, q)]
                new[(p, p)] = a[(p, p)] - tan * off
                new[(q, q)] = a[(q, q)] + tan * off
                new[(p, q)] = zero
                x, y = vec[p], vec[q]
                vec[p], vec[q] = cos * x - sin * y, sin * x + cos * y
                for r, s in pairs[n + 1 :]:
                    cos2, sin2, _t = turn[(r, s)]
                    half = []
                    for i in (p, q):
                        x, y = get(i, r), get(i, s)
                        half.append((cos2 * x - sin2 * y, sin2 * x + cos2 * y))
                    for j, x, y in ((r, half[0][0], half[1][0]), (s, half[0][1], half[1][1])):
                        new[tuple(sorted((p, j)))] = cos * x - sin * y
                        new[tuple(sorted((q, j)))] = sin * x + cos * y
            a = new
        return tuple(a[pair] for pair in PAIRS), tuple(vec)

    start = (tuple(a[pair] for pair in PAIRS), tuple(vec))
    flat_a, flat_v = lax.fori_loop(0, SWEEPS, sweep, start)
    a = dict(zip(PAIRS, flat_a))
    for mode in range(8):
        mu_ref[mode : mode + 1, :] = jnp.minimum(a[(mode, mode)] * (1.0 / unit), 0.0)[0:1]
        mix_ref[8 * mode : 8 * mode + 8, :] = flat_v[mode] * scale
        unmix_ref[pl.ds(mode, 8, stride=8), :] = flat_v[mode] / scale


def iota(shape, axis):
    return lax.broadcasted_iota(jnp.int32, shape, axis)


def divergence_kernel(
    gx_ref, thick_ref, u_hbm, v_hbm, w_hbm, out_ref, unmix_ref, mu_ref,
    mix_ref, u_ref, v_ref, w_ref, last_ref, sum_ref, sems,
):
    def copies(step):
        rows = pl.ds(128 * step, 128)
        return [
            pltpu.make_async_copy(src.at[:, rows, :], dst.at[:, rows, :], sems.at[n, step])
            for n, (src, dst) in enumerate(((u_hbm, u_ref), (v_hbm, v_ref), (w_hbm, w_ref)))
        ]

    for step in range(4):
        for copy in copies(step):
            copy.start()
    vertical_modes(thick_ref, mix_ref, unmix_ref, mu_ref)

    last_ref[...] = jnp.zeros((64, 128), f32)
    sum_ref[...] = jnp.zeros((64, 128), f32)
    lane = iota((16, 128), 1)
    row = iota((16, 128), 0)
    lanes = iota((128, 128), 1)
    ones = jnp.ones((1, 128), f32)
    inverse = [1.0 / (ones * thick_ref[k]) for k in range(8)]

    def block(step, carry):
        for copy in copies(step):
            copy.wait()
        wall = jnp.logical_and(gx_ref[0] == 7, step == 3)
        base = pl.multiple_of(step * 128, 128)
        for sub in range(8):
            rows = pl.ds(base + 16 * sub, 16)
            div = []
            below = None
            for k in range(8):
                u = u_ref[k, rows, :]
                if sub == 7:
                    u = jnp.where(jnp.logical_and(wall, row == 15), 0.0, u)
                prev = pltpu.roll(u, 1, axis=0)
                prev = jnp.where(row == 0, last_ref[8 * k : 8 * k + 1, :], prev)
                last_ref[8 * k : 8 * k + 1, :] = u[15:16]
                v = v_ref[k, rows, :]
                back = jnp.where(lane == 0, 0.0, pltpu.roll(v, 1, axis=1))
                if k < 7:
                    w = w_ref[k, rows, :]
                    up = w if below is None else w - below
                    below = w
                else:
                    up = -below
                rise = up * inverse[k]
                sum_ref[8 * k : 8 * k + 8, :] += rise[0:8] + rise[8:16]
                div.append((u - prev) + (v - back) + rise)
            for mode in range(8):
                acc = div[0] * mix_ref[8 * mode : 8 * mode + 1, :]
                for k in range(1, 8):
                    acc = acc + div[k] * mix_ref[8 * mode + k : 8 * mode + k + 1, :]
                out_ref[mode, rows, :] = acc

        edge = jnp.zeros((128, 128), f32)
        for k in range(8):
            edge = jnp.where(lanes == k, pltpu.roll(v_ref[k, pl.ds(base, 128), :], k + 1, axis=1), edge)
        edge = edge.T
        for mode in range(8):
            acc = edge[0:1] * mix_ref[8 * mode : 8 * mode + 1, :]
            for k in range(1, 8):
                acc = acc + edge[k : k + 1] * mix_ref[8 * mode + k : 8 * mode + k + 1, :]
            out_ref[mode, pl.ds(513 + step, 1), :] = -acc
        return carry

    lax.fori_loop(0, 4, block, 0)

    lane1 = iota((1, 128), 1)
    totals = jnp.zeros((1, 128), f32)
    for k in range(8):
        part = jnp.sum(sum_ref[8 * k : 8 * k + 8, :], axis=0, keepdims=True)
        part = jnp.sum(part, axis=1, keepdims=True)
        totals = jnp.where(lane1 == k, part, totals)
    for mode in range(8):
        acc = last_ref[0:1, :] * mix_ref[8 * mode : 8 * mode + 1, :]
        for k in range(1, 8):
            acc = acc + last_ref[8 * k : 8 * k + 1, :] * mix_ref[8 * mode + k : 8 * mode + k + 1, :]
        out_ref[mode, 512:513, :] = acc
        out_ref[mode, 517:518, :] = totals
        out_ref[mode, 518:520, :] = jnp.zeros((2, 128), f32)


def eigen_table(sines, mu_row, with_first):
    eigen = mu_row - 4.0 * sines
    if with_first:
        first = jnp.logical_and(iota(sines.shape, 0) == 0, iota(sines.shape, 1) == 0)
        eigen = jnp.where(first, -1.0, eigen)
    return eigen


def forward_kernel(
    gx_ref, mu_ref, sines_ref, tc_ref, ts_ref, common_ref, first_ref, in_ref, out_ref, small_ref,
    south_ref, north_ref, grid_ref, y_ref, raw_ref, side_ref, turn_ref,
):
    row8 = iota((8, 128), 0)
    row128 = iota((128, 128), 0)
    for s in range(8):
        for part in range(4):
            tile = in_ref[s, 128 * part : 128 * part + 128, :]
            if part == 0 and s > 0:
                tile = jnp.where(row128 == 0, tile - in_ref[s - 1, 512:513, :], tile)
            grid_ref[4 * s + part, 0:128, :] = tile.T
            ghost = in_ref[s, 513 + part : 514 + part, :]
            grid_ref[4 * s + part, 128:136, :] = jnp.where(row8 == 0, ghost, 0.0)

    def group(i, carry):
        start = pl.multiple_of(i * 8, 8)
        y = forward_classes([grid_ref[g, pl.ds(start, 8), :] for g in range(32)])
        y_ref[pl.ds(start, 8), 0:128] = y[0][0]
        y_ref[pl.ds(start, 8), 128:256] = y[0][1]
        for c in range(1, 32):
            re, im = y[c]
            tc, ts = tc_ref[c : c + 1, :], ts_ref[c : c + 1, :]
            rows = pl.ds(start + ROWS * c, 8)
            y_ref[rows, 0:128] = re * tc + im * ts
            y_ref[rows, 128:256] = im * tc - re * ts
        return carry

    lax.fori_loop(0, ROWS // 8, group, 0)

    batch = BATCH * ROWS

    def product(n, carry):
        start = pl.multiple_of(n * batch, 8)
        raw_ref[pl.ds(start, batch), :] = forward_product(y_ref[pl.ds(start, batch), :], common_ref)
        return carry

    lax.fori_loop(0, 32 // BATCH, product, 0)
    raw_ref[0:144, :] = jnp.where(
        iota((144, 128), 0) < ROWS, forward_product(y_ref[0:144, :], first_ref), raw_ref[0:144, :]
    )

    line = raw_ref[0:128, :].T[0:1]
    ghost_line = raw_ref[128:129, :]

    eigen = eigen_table(sines_ref[...], mu_ref[pl.ds(gx_ref[0], 1), :], True)
    rho, gap, _ = decay(eigen)
    ghost = raw_ref[pl.ds(128, 32, stride=ROWS), :]

    def from_north(n, b):
        j = 127 - n
        side_ref[pl.ds(j, 32, stride=ROWS), :] = rho * b
        return raw_ref[pl.ds(j, 32, stride=ROWS), :] + (b - gap * b)

    b = lax.fori_loop(0, 128, from_north, ghost, unroll=8)

    def from_south(j, f):
        f = raw_ref[pl.ds(j, 32, stride=ROWS), :] + (f - gap * f)
        out_ref[pl.ds(j, 32, stride=ROWS), :] = f + side_ref[pl.ds(j, 32, stride=ROWS), :]
        return f

    f = lax.fori_loop(0, 128, from_south, jnp.zeros((32, 128), f32), unroll=8)
    out_ref[pl.ds(128, 32, stride=ROWS), :] = rho * f + ghost
    for r in range(129, ROWS):
        out_ref[pl.ds(r, 32, stride=ROWS), :] = jnp.zeros((32, 128), f32)

    totals = in_ref[0, 517:518, :]
    for s in range(1, 8):
        totals = totals + in_ref[s, 517:518, :]
    f = f + ghost / rho
    south_ref[...] = f
    north_ref[...] = b
    turn_ref[0:32, :] = f
    turn_ref[32:64, :] = b
    turn_ref[64:128, :] = jnp.zeros((64, 128), f32)
    turn_ref[...] = turn_ref[...].T
    turn_ref[4:8, :] = turn_ref[64:68, :]
    lane1 = iota((1, 128), 1)
    extra = [pltpu.roll(line, 64, axis=1), line, pltpu.roll(totals, 64, axis=1), pltpu.roll(ghost_line, 64, axis=1)]
    for r in range(4):
        turn_ref[r : r + 1, :] = jnp.where(lane1 < 64, turn_ref[r : r + 1, :], extra[r])
    for d in range(32):
        small_ref[8 * d : 8 * d + 8, :] = turn_ref[0:8, :]


def line_kernel(
    gx_ref, gy_ref, thick_ref, mu_ref, slow_ref, c32_ref, s32_ref, tc_ref, ts_ref, c128_ref, s128_ref, lam_ref,
    in_ref, out_ref, turn_ref,
):
    def times(a, b):
        return jnp.dot(a, b, precision=highest, preferred_element_type=f32)

    own = gy_ref[0]
    eigen = mu_ref[pl.ds(gx_ref[0], 1), :] - 4.0 * slow_ref[...]
    lane8 = iota((8, 128), 1)
    first = jnp.logical_and(iota((8, 128), 0) == 0, lane8 % 32 == 0)
    _, gap, _ = decay(jnp.where(first, -1.0, eigen))
    gap_block = doubled(gap, 7)
    around = 1.0 / doubled(gap_block, 5)
    c = jnp.zeros((8, 128), f32)
    h = jnp.zeros((8, 128), f32)
    for e in range(32, 0, -1):
        c = in_ref[pl.ds(pl.multiple_of((own + 32 - e) % 32 * 8, 8), 8), :] + (c - gap_block * c)
        h = in_ref[pl.ds(pl.multiple_of((own + e) % 32 * 8, 8), 8), :] + (h - gap_block * h)
    carry = jnp.where(lane8 < 32, c, h) * around
    turn_ref[...] = jnp.zeros((128, 128), f32)
    turn_ref[0:4, :] = carry[0:4]
    turn_ref[64:68, :] = carry[4:8]
    out_ref[40:104, :] = turn_ref[...].T[0:64]

    lane32 = iota((32, 128), 1)
    line = jnp.where(
        lane32 < 64,
        pltpu.roll(in_ref[pl.ds(0, 32, stride=8), :], 64, axis=1),
        in_ref[pl.ds(1, 32, stride=8), :],
    )
    ghost = pltpu.roll(in_ref[pl.ds(3, 32, stride=8), :], 64, axis=1)
    at_first = iota((32, 128), 1) == 0
    line = line + jnp.where(at_first, pltpu.roll(ghost, 1, axis=0), 0.0)
    c32, s32 = c32_ref[...], s32_ref[...]
    tc, ts = tc_ref[...], ts_ref[...]
    c128, s128 = c128_ref[...], s128_ref[...]
    re, im = times(c32, line), -times(s32, line)
    re, im = re * tc + im * ts, im * tc - re * ts
    re, im = times(re, c128) + times(im, s128), times(im, c128) - times(re, s128)
    mean = jnp.logical_and(iota((32, 128), 0) == 0, at_first)
    eigen = mu_ref[pl.ds(gx_ref[0], 1), :] + lam_ref[...]
    gain = jnp.where(mean, 0.0, (1.0 / NY) / jnp.where(mean, 1.0, eigen))
    re, im = re * gain, im * gain
    re, im = times(re, c128) - times(im, s128), times(im, c128) + times(re, s128)
    re, im = re * tc - im * ts, im * tc + re * ts
    out_ref[0:32, :] = times(c32, re) - times(s32, im)

    totals = jnp.sum(in_ref[pl.ds(2, 32, stride=8), :], axis=0, keepdims=True)
    totals = pltpu.roll(totals, 64, axis=1)
    lane = iota((1, 128), 1)
    ones = jnp.ones((1, 128), f32)
    rhs = [ones * jnp.sum(jnp.where(lane == k, totals, 0.0), axis=1, keepdims=True) for k in range(8)]
    t = [ones * thick_ref[k] for k in range(8)]
    centre = [0.5 * (t[k] + t[k + 1]) for k in range(7)]
    zero = jnp.zeros((1, 128), f32)
    upper = [1.0 / (t[k] * centre[k]) for k in range(7)] + [zero]
    lower = [zero] + [1.0 / (t[k] * centre[k - 1]) for k in range(1, 8)]
    reduced, ratio = [], []
    excess = zero
    for k in range(8):
        if k == 0:
            excess = -upper[0]
            top = rhs[0]
        else:
            excess = lower[k] * excess / (upper[k - 1] - excess)
            top = rhs[k] - lower[k] * reduced[-1]
        pivot = excess - upper[k]
        reduced.append(top / pivot)
        ratio.append(upper[k] / pivot)
    value = zero
    for k in reversed(range(8)):
        value = reduced[k] - ratio[k] * value
        out_ref[32 + k : 33 + k, :] = value * (1.0 / NX) * (1.0 / NY)


def backward_kernel(
    gx_ref, gy_ref, mu_ref, sines_ref, tc_ref, ts_ref, common_ref, first_ref, line_ref, south_ref,
    north_ref, in_ref, out_ref, half_ref, p_ref, z_ref, grid_ref,
):
    eigen = eigen_table(sines_ref[...], mu_ref[pl.ds(gx_ref[0], 1), :], True)
    rho, gap, factor = decay(eigen)
    at_zero = jnp.logical_and(iota((32, 128), 0) == 0, iota((32, 128), 1) == 0)
    factor = factor * jnp.where(at_zero, 1.0 / NX, 2.0 / NX)
    slow = iota((32, 128), 1) % 64 < 4
    south = jnp.where(slow, line_ref[40:72, :], south_ref[...])
    north = jnp.where(slow, line_ref[72:104, :], north_ref[...])

    def from_south(j, c):
        c = c - gap * c
        half_ref[pl.ds(j, 32, stride=ROWS), :] = in_ref[pl.ds(j, 32, stride=ROWS), :] + c
        return c

    c = lax.fori_loop(0, 128, from_south, south, unroll=8)
    c = c - gap * c
    p_ref[pl.ds(128, 32, stride=ROWS), :] = (in_ref[pl.ds(128, 32, stride=ROWS), :] + c + north) * factor

    def from_north(n, h):
        j = 127 - n
        h = h - gap * h
        p_ref[pl.ds(j, 32, stride=ROWS), :] = (half_ref[pl.ds(j, 32, stride=ROWS), :] + h) * factor
        return h

    lax.fori_loop(0, 128, from_north, north, unroll=8)
    for r in range(129, ROWS):
        p_ref[pl.ds(r, 32, stride=ROWS), :] = jnp.zeros((32, 128), f32)

    own = gy_ref[0]
    line = line_ref[pl.ds(own, 1), :] * (1.0 / NX)
    after = line_ref[pl.ds((own + 1) % 32, 1), :] * (1.0 / NX)
    lane128 = iota((128, 128), 1)
    column = jnp.where(iota((128, 128), 0) == 0, line, 0.0).T
    p_ref[0:128, :] = jnp.where(lane128 == 0, column, p_ref[0:128, :])
    lane1 = iota((1, 128), 1)
    p_ref[128:129, :] = jnp.where(lane1 == 0, after, p_ref[128:129, :])

    batch = BATCH * ROWS

    def product(n, carry):
        start = pl.multiple_of(n * batch, 8)
        z_ref[pl.ds(start, batch), :] = backward_product(p_ref[pl.ds(start, batch), :], common_ref)
        return carry

    lax.fori_loop(0, 32 // BATCH, product, 0)
    z_ref[0:ROWS, :] = backward_product(p_ref[0:144, :], first_ref)[0:ROWS]

    def group(i, carry):
        start = pl.multiple_of(i * 8, 8)
        rows = pl.ds(start, 8)
        h = [(z_ref[rows, 0:128], z_ref[rows, 128:256])]
        for c in range(1, 32):
            part = pl.ds(start + ROWS * c, 8)
            re, im = z_ref[part, 0:128], z_ref[part, 128:256]
            tc, ts = tc_ref[c : c + 1, :], ts_ref[c : c + 1, :]
            h.append((re * tc - im * ts, im * tc + re * ts))
        x = backward_classes(h)
        for g in range(32):
            grid_ref[g, rows, :] = x[g]
        return carry

    lax.fori_loop(0, ROWS // 8, group, 0)

    for s in range(8):
        for part in range(4):
            tile = grid_ref[4 * s + part, 0:128, :].T
            out_ref[s, 128 * part : 128 * part + 128, :] = tile
            if part == 0 and s > 0:
                out_ref[s - 1, 512:513, :] = tile[0:1]
            out_ref[s, 513 + part : 514 + part, :] = grid_ref[4 * s + part, 128:129, :]
        out_ref[s, 517:520, :] = jnp.zeros((3, 128), f32)
    out_ref[7, 512:513, :] = jnp.zeros((1, 128), f32)


def gradient_kernel(
    gx_ref, thick_ref, unmix_ref, line_ref, p_ref, u_ref, v_ref, w_ref, uo_ref, vo_ref, wo_ref, press_ref, edge_ref
):
    step = pl.program_id(0)
    base = pl.multiple_of(step * 128, 128)
    wall = jnp.logical_and(gx_ref[0] == 7, step == 3)
    edge_ref[...] = jnp.zeros((128, 128), f32)
    for k in range(8):
        acc = p_ref[0, pl.ds(513 + step, 1), :] * unmix_ref[8 * k : 8 * k + 1, :]
        for mode in range(1, 8):
            acc = acc + p_ref[mode, pl.ds(513 + step, 1), :] * unmix_ref[8 * k + mode : 8 * k + mode + 1, :]
        edge_ref[k : k + 1, :] = acc
    edge_ref[...] = edge_ref[...].T
    for sub in range(17):
        parts = [p_ref[mode, pl.ds(base + 8 * sub, 8), :] for mode in range(8)]
        for k in range(8):
            acc = parts[0] * unmix_ref[8 * k : 8 * k + 1, :]
            for mode in range(1, 8):
                acc = acc + parts[mode] * unmix_ref[8 * k + mode : 8 * k + mode + 1, :]
            press_ref[k, 8 * sub : 8 * sub + 8, :] = acc
    lane = iota((16, 128), 1)
    row = iota((16, 128), 0)
    ones = jnp.ones((1, 128), f32)
    t = [ones * thick_ref[k] for k in range(8)]
    inverse = [2.0 / (t[k] + t[k + 1]) for k in range(7)]
    drift = [(line_ref[33 + k : 34 + k, :] - line_ref[32 + k : 33 + k, :]) * inverse[k] for k in range(7)]
    for sub in range(8):
        rows = slice(16 * sub, 16 * sub + 16)
        edge = edge_ref[rows, :]
        for k in range(8):
            p = press_ref[k, rows, :]
            east = press_ref[k, 16 * sub + 1 : 16 * sub + 17, :]
            u = u_ref[k, rows, :] - (east - p)
            if sub == 7:
                u = jnp.where(jnp.logical_and(wall, row == 15), 0.0, u)
            uo_ref[k, rows, :] = u
            north = jnp.where(lane == 127, pltpu.roll(edge, 127 - k, axis=1), pltpu.roll(p, 127, axis=1))
            vo_ref[k, rows, :] = v_ref[k, rows, :] - (north - p)
            if k < 7:
                wo_ref[k, rows, :] = w_ref[k, rows, :] - ((press_ref[k + 1, rows, :] - p) * inverse[k] + drift[k])
            else:
                wo_ref[k, rows, :] = jnp.zeros((16, 128), f32)


SMEM = pl.BlockSpec(memory_space=pltpu.SMEM)
VMEM = pl.BlockSpec(memory_space=pltpu.VMEM)


def params(mib):
    return pltpu.CompilerParams(vmem_limit_bytes=mib * 2**20)


def whole(shape):
    return pl.BlockSpec(shape, lambda i: (0,) * len(shape))


def on_device(u_vel, v_vel, w_vel, thickness):
    gx = lax.axis_index("gx").astype(jnp.int32)[None]
    gy = lax.axis_index("gy").astype(jnp.int32)[None]
    common, first, tc, ts = dct_tables()
    sines = const(np.sin(math.pi * class_modes() / 8192) ** 2)
    tables = (sines, const(tc), const(ts))
    shape = jax.ShapeDtypeStruct

    block = pl.BlockSpec((8, 128, 128), lambda i: (0, i, 0))
    field = (8, PAY, 128)
    local_field = pltpu.VMEM((8, LX, 128), f32)
    packed, unmix, mu = pl.pallas_call(
        divergence_kernel,
        out_shape=(shape(field, f32), shape((64, 128), f32), shape((8, 128), f32)),
        in_specs=[SMEM, SMEM] + [pl.BlockSpec(memory_space=pltpu.HBM)] * 3,
        out_specs=(VMEM, VMEM, VMEM),
        scratch_shapes=[
            pltpu.VMEM((64, 128), f32),
            local_field,
            local_field,
            local_field,
            pltpu.VMEM((64, 128), f32),
            pltpu.VMEM((64, 128), f32),
            pltpu.SemaphoreType.DMA((3, 4)),
        ],
        compiler_params=params(12),
        name="divergence",
    )(gx, thickness, *[pltpu.with_memory_space_constraint(x, pltpu.HBM) for x in (u_vel, v_vel, w_vel)])
    packed = lax.all_to_all(packed, "gx", split_axis=0, concat_axis=0, tiled=True)

    rows = shape((32, 128), f32)
    local, small, south, north = pl.pallas_call(
        forward_kernel,
        out_shape=(shape((32 * ROWS, 128), f32), shape((256, 128), f32), rows, rows),
        in_specs=[SMEM] + [VMEM] * 7,
        out_specs=(VMEM, VMEM, VMEM, VMEM),
        scratch_shapes=[
            pltpu.VMEM((32, ROWS, 128), f32),
            pltpu.VMEM((32 * ROWS, 256), f32),
            pltpu.VMEM((32 * ROWS, 128), f32),
            pltpu.VMEM((32 * ROWS, 128), f32),
            pltpu.VMEM((128, 128), f32),
        ],
        compiler_params=params(20),
        name="forward",
    )(gx, mu, *tables, forward_weights(common), forward_weights(first), packed)
    small = lax.all_to_all(small, "gy", split_axis=0, concat_axis=0, tiled=True)

    parts = lax.axis_size("gy")
    south = lax.ppermute(south, "gy", [(i, (i + 1) % parts) for i in range(parts)])
    north = lax.ppermute(north, "gy", [(i, (i - 1) % parts) for i in range(parts)])
    line = pl.pallas_call(
        line_kernel,
        out_shape=shape((104, 128), f32),
        in_specs=[SMEM, SMEM, SMEM] + [VMEM] * 10,
        out_specs=VMEM,
        scratch_shapes=[pltpu.VMEM((128, 128), f32)],
        compiler_params=params(4),
        name="line",
    )(gx, gy, thickness, mu, const(slow_table()), *[const(x) for x in line_tables()], small)

    packed = pl.pallas_call(
        backward_kernel,
        out_shape=shape(field, f32),
        in_specs=[SMEM, SMEM] + [VMEM] * 10,
        out_specs=VMEM,
        compiler_params=params(20),
        scratch_shapes=[
            pltpu.VMEM((32 * ROWS, 128), f32),
            pltpu.VMEM((32 * ROWS, 128), f32),
            pltpu.VMEM((32 * ROWS, 256), f32),
            pltpu.VMEM((32, ROWS, 128), f32),
        ],
        name="backward",
    )(gx, gy, mu, *tables, backward_weights(common), backward_weights(first), line, south, north, local)
    packed = lax.all_to_all(packed, "gx", split_axis=0, concat_axis=0, tiled=True)

    out = shape((8, LX, 128), f32)
    return pl.pallas_call(
        gradient_kernel,
        out_shape=(out, out, out),
        grid=(4,),
        in_specs=[SMEM, SMEM, whole((64, 128)), whole((104, 128)), whole(field), block, block, block],
        out_specs=(block, block, block),
        scratch_shapes=[pltpu.VMEM((8, 136, 128), f32), pltpu.VMEM((128, 128), f32)],
        compiler_params=params(16),
        name="gradient",
    )(gx, thickness, unmix, line, packed, u_vel, v_vel, w_vel)


def solution(mesh):
    return jax.shard_map(
        on_device,
        mesh=mesh,
        in_specs=(P(None, "gx", "gy"), P(None, "gx", "gy"), P(None, "gx", "gy"), P()),
        out_specs=(P(None, "gx", "gy"), P(None, "gx", "gy"), P(None, "gx", "gy")),
        check_vma=False,
    )
```
